512 devices in a mesh: src: 128 (over y, z, core), freq: 4 (over x).
Axes of the slice: x: 4, y: 8, z: 8, core: 2. Of those that a mesh axis runs over, the one named last changes fastest.
Arguments:
- pupil_block: bfloat16 [32768, 1024], P('src'), may hold values from -6 to 6
- source_on: int32 [32768], P('src'), may hold values 0 or 1
- offsets: int32 [2, 32768], P(None, 'src'), may hold values from 0 to 96, as said below
- omega: bfloat16 [32768, 64], P('src'), may hold values from -6 to 6
Outputs:
- kernels: float32 [16384, 64], P('freq')
The draws below stay inside these ranges and needn't reach their ends.
Inputs may be any that keep to these rules, and one draw needn't show every extreme that they name: offsets[0, s] and offsets[1, s] place source point s's whole window inside the grid.
All inputs are finite; a program needn't handle non-finite values. No bound on the sum of `source_on` on one device may be relied on, other than what follows from the above.
Results may differ from the reference program's by a relative error of at most 0.0033.
Values may be sent and summed in bfloat16 or wider, within the bound.
A program may use at most 64 MiB of HBM per device.

```python
import jax
import jax.numpy as jnp
from jax import lax

G = 128
PB = 32
K = 64
S_DEV = 256
ITERS = 3
S = 32768
N_SRC = 128


def draw_offsets(key, part):
    highest = G - PB
    row_key = jax.random.fold_in(key, 11)
    col_key = jax.random.fold_in(key, 12)
    row_start = jnp.clip(jax.random.randint(row_key, (S,), -4, highest + 5), 0, highest)
    col_start = jnp.clip(jax.random.randint(col_key, (S,), -4, highest + 5), 0, highest)
    row_start = row_start.at[0].set(0).at[1].set(highest)
    col_start = col_start.at[0].set(highest).at[1].set(0)
    return jnp.stack([row_start, col_start]).astype(jnp.int32)


def plant(result, own_key, low, top_value):
    dims = result.shape
    index_at = [jax.random.randint(jax.random.fold_in(own_key, axis), (), 0, dims[axis]) for axis in range(len(dims))]
    result = result.at[tuple(index_at)].set(low)
    longest = dims.index(max(dims))
    index_at[longest] = (index_at[longest] + 1) % dims[longest]
    return result.at[tuple(index_at)].set(top_value)


def levels(own_key, extent, cuts, low, high):
    def one(position, shards_of):
        draws = jax.random.uniform(jax.random.fold_in(jax.random.fold_in(own_key, 6), position), (shards_of,), jnp.float32, low / len(cuts), high / len(cuts))
        return jnp.repeat(jnp.exp(draws), extent[position] // shards_of).reshape((-1,) + (1,) * (len(extent) - position - 1))

    loudness = one(*cuts[0])
    for cut in cuts[1:]:
        loudness = loudness * one(*cut)
    return loudness


def centred(rng, dims, width, bound, split=(), kind=jnp.bfloat16):
    values = jax.random.normal(rng, dims, jnp.float32) * width
    if len(split) > 0:
        values = levels(rng, dims, split, -0.22, 0.18) * values
    return jnp.clip(values, min=-bound, max=bound).astype(kind)


def setup_inputs(seed: int = 0) -> dict:
    splits = jax.random.split(jax.random.key(seed), 5)
    return {
        "pupil_block": centred(splits[0], (S, PB * PB), 1.0, 6.0, ((0, 128),)),
        "source_on": plant((jax.random.randint(splits[1], (S,), 0, 3) < 2).astype(jnp.int32), jax.random.fold_in(splits[1], 1), 0, 1),
        "offsets": draw_offsets(jax.random.fold_in(splits[4], 71), 0),
        "omega": centred(splits[3], (S, K), 1.0, 6.0, ((0, 128),)),
    }


def assemble(pupil, on_flags, row_offset, col_offset):
    points = pupil.shape[0]
    inner_idx = jnp.arange(PB, dtype=jnp.int32)
    target = ((row_offset[:, None, None] + inner_idx[None, :, None]) * G + col_offset[:, None, None] + inner_idx[None, None, :]).reshape(points, PB * PB)
    column = jnp.broadcast_to(jnp.arange(points, dtype=jnp.int32)[:, None], (points, PB * PB))
    values = pupil * on_flags.astype(pupil.dtype)[:, None]
    return jnp.zeros((G * G, points), pupil.dtype).at[target, column].set(values)

def reference(pupil_block, source_on, offsets, omega):
    blocks = pupil_block.reshape(N_SRC, S_DEV, PB * PB)
    flag_table = source_on.reshape(N_SRC, S_DEV)
    row_table = offsets[0].reshape(N_SRC, S_DEV)
    col_table = offsets[1].reshape(N_SRC, S_DEV)
    sketch = omega.reshape(N_SRC, S_DEV, K)
    current = None
    kernels = None
    for iteration in range(ITERS):

        def accumulate(running, pieces):
            pupil, on_flags, row_offset, col_offset, sketch_part = pieces
            shift_matrix = assemble(pupil, on_flags, row_offset, col_offset)
            if iteration == 0:
                coupled = sketch_part
            else:
                coupled = jnp.dot(shift_matrix.T.astype(jnp.float32), current.astype(jnp.float32), preferred_element_type=jnp.float32).astype(jnp.bfloat16)
            return (running + jnp.dot(shift_matrix.astype(jnp.float32), coupled.astype(jnp.float32), preferred_element_type=jnp.float32), None)
        images, unused = lax.scan(accumulate, jnp.zeros((G * G, K), jnp.float32), (blocks, flag_table, row_table, col_table, sketch))
        gram_sum = jnp.dot(images.T.astype(jnp.float32), images.astype(jnp.float32), precision=lax.Precision.HIGHEST, preferred_element_type=jnp.float32) / (G * G)
        factor = jnp.linalg.cholesky(gram_sum)
        kernels = jax.scipy.linalg.solve_triangular(factor, images.T, lower=True).T
        current = kernels.astype(jnp.bfloat16)
    return kernels
```

```python
import functools

import jax
import jax.numpy as jnp
from jax import lax
from jax.experimental import pallas as pl
from jax.experimental.pallas import tpu as pltpu
from jax.sharding import Mesh
from jax.sharding import PartitionSpec as P

G = 128
PB = 32
ITERS = 3
LANES = 128
SRC = ("src_0", "src_1", "src_2")
MESH_ID = pl.DeviceIdType.MESH


def split2(value):
    high = value.astype(jnp.bfloat16)
    low = (value - high.astype(jnp.float32)).astype(jnp.bfloat16)
    return high, low


def dot_nn(left, right):
    return lax.dot_general(
        left, right, (((1,), (0,)), ((), ())), preferred_element_type=jnp.float32
    )


def dot_nt(left, right):
    return lax.dot_general(
        left, right, (((1,), (1,)), ((), ())), preferred_element_type=jnp.float32
    )


def apply_factor(inv_high, inv_low, value):
    high, low = split2(value)
    return dot_nn(inv_high, high) + (dot_nn(inv_high, low) + dot_nn(inv_low, high))


def place_windows(pupil_ref, off_ref, on_ref, meta_ref, a_ref, a_row, base_row, rows):
    points = pupil_ref.shape[0]
    per = LANES // PB
    chunk = 16

    def spread(line):
        return jnp.transpose(jnp.broadcast_to(line, (LANES, points)))

    meta_ref[0] = spread(off_ref[0:1, :])
    meta_ref[1] = spread(off_ref[1:2, :])
    meta_ref[2] = spread(on_ref[0:1, :])

    def block(index, carry):
        s0 = pl.multiple_of(index * chunk, chunk)
        row_off = meta_ref[0, pl.ds(s0, chunk), :]
        col_off = meta_ref[1, pl.ds(s0, chunk), :]
        lit = meta_ref[2, pl.ds(s0, chunk), :].astype(jnp.float32)
        lane = lax.broadcasted_iota(jnp.int32, (chunk, LANES), 1)
        shift = jnp.clip(base_row - row_off, -rows, PB) + rows
        window = pupil_ref[pl.ds(s0, chunk), :].astype(jnp.float32)
        tiles = [None] * (rows // per)
        tiles += [window[:, i * LANES : (i + 1) * LANES] * lit for i in range(PB // per)]
        tiles += [None] * (rows // per)
        zero = jnp.zeros((chunk, LANES), jnp.float32)

        def pick(mask, taken, kept):
            if taken is None and kept is None:
                return None
            return jnp.where(mask, zero if taken is None else taken, zero if kept is None else kept)

        kept_tiles = rows // per + 1
        for bit in reversed(range(((rows + PB) // per).bit_length())):
            step = 1 << bit
            mask = (shift & (step * per)) != 0
            count = kept_tiles + step - 1
            at = lambda i: tiles[i] if i < len(tiles) else None
            tiles = [pick(mask, at(i + step), at(i)) for i in range(count)]
        for step in (2, 1):
            mask = (shift & step) != 0
            turned = [None if t is None else pltpu.roll(t, LANES - PB * step, 1) for t in tiles]
            turned.append(None)
            inside = lane < LANES - PB * step
            moved = [pick(inside, turned[i], turned[i + 1]) for i in range(len(tiles))]
            tiles = [pick(mask, moved[i], tiles[i]) for i in range(len(tiles))]
        tiles = tiles[: rows // per]
        for bit in range(LANES.bit_length() - 1):
            mask = (col_off & (1 << bit)) != 0
            tiles = [jnp.where(mask, pltpu.roll(t, 1 << bit, 1), t) for t in tiles]
        inner = lane - col_off
        covered = (inner >= 0) & (inner < PB)
        for row in range(rows):
            tile, group = tiles[row // per], row % per
            if group:
                tile = pltpu.roll(tile, LANES - PB * group, 1)
            a_ref[pl.ds(a_row + s0, chunk), row * LANES : (row + 1) * LANES] = jnp.where(
                covered, tile, 0.0
            ).astype(jnp.bfloat16)
        return carry

    lax.fori_loop(0, points // chunk, block, 0)


def inverse_factor(packed, size):
    half = size // 2
    whole = jnp.concatenate([pltpu.roll(packed, size, 1), packed], axis=0)
    lane = lax.broadcasted_iota(jnp.int32, (8, LANES), 1)
    sub = lax.broadcasted_iota(jnp.int32, (8, LANES), 0)
    tiles = []
    for t in range(size // 8):
        eye = jnp.where(lane == sub + 8 * t, 1.0, 0.0)
        tiles.append(jnp.where(lane < size, eye, whole[8 * t : 8 * t + 8]))
    for k in range(size):
        home, inside = k // 8, k % 8
        line = tiles[home][inside : inside + 1, :]
        scaled = line * (1.0 / line[:, size + k : size + k + 1])
        for t in range(home, size // 8):
            column = tiles[t][:, size + k : size + k + 1]
            if t == home:
                column = jnp.where(sub[:, :1] > inside, column, 0.0)
            tiles[t] = tiles[t] - column * scaled
    done = []
    for t in range(size // 8):
        pivot = jnp.sum(jnp.where(lane == sub + (8 * t + size), tiles[t], 0.0), axis=1, keepdims=True)
        done.append(tiles[t] * lax.rsqrt(pivot))
    return jnp.concatenate(done, axis=0)[:, :size]


def kernel(
    sizes, pupil_ref, on_ref, off_ref, omega_ref, out_ref,
    pupil_far, on_far, off_far, meta, a_ref, cpl_own, cpl_far,
    part, got1, sum1, got2, sum2, img, split, gram_out, gram_in, w_far, w_far_in, w_own, w_in,
    setup_send, setup_recv, st_send, st_recv, gram_send, gram_recv, w_send, w_recv, x_send, x_recv,
    c_send, c_recv, f_send, f_recv,
):
    n_y, n_z, n_c, n_x = sizes
    my_y, my_z = lax.axis_index("src_0"), lax.axis_index("src_1")
    my_c, my_x = lax.axis_index("src_2"), lax.axis_index("freq")
    other = {"src_2": 1 - my_c}
    rows = G // (n_x * n_c)
    size = omega_ref.shape[0]
    points = pupil_ref.shape[0]
    half = rows * G // 2
    axes = ("src_0", "src_1")
    count = (n_y, n_z)
    mine = (my_y, my_z)

    def offsets_far_first(n):
        return sorted(range(1, n), key=lambda d: (-min(d, n - d), d))

    group = [(dx, dc) for dx in range(n_x) for dc in range(n_c) if dx or dc]

    def group_peer(dx, dc):
        peer_x = lax.rem(my_x + dx, n_x)
        peer_c = lax.rem(my_c + dc, n_c)
        return peer_x, peer_c

    barrier = pltpu.get_barrier_semaphore()
    for a in range(2):
        for d in range(1, count[a]):
            pl.semaphore_signal(
                barrier, inc=1, device_id={axes[a]: lax.rem(mine[a] + d, count[a])},
                device_id_type=MESH_ID,
            )
    for dx, dc in group:
        peer_x, peer_c = group_peer(dx, dc)
        pl.semaphore_signal(
            barrier, inc=1, device_id={"freq": peer_x, "src_2": peer_c}, device_id_type=MESH_ID
        )
    pl.semaphore_wait(barrier, n_y - 1 + n_z - 1 + len(group))

    def remote(src, dst, send, recv, device):
        return pltpu.make_async_remote_copy(
            src_ref=src, dst_ref=dst, send_sem=send, recv_sem=recv,
            device_id=device, device_id_type=MESH_ID,
        )

    setup = [
        remote(src, dst, setup_send.at[i], setup_recv.at[i], other)
        for i, (src, dst) in enumerate(
            ((off_ref, off_far), (on_ref, on_far), (omega_ref, cpl_far.at[0]), (pupil_ref, pupil_far))
        )
    ]
    for copy in setup:
        copy.start()
    base_row = my_x * (rows * n_c) + my_c * rows
    place_windows(pupil_ref, off_ref, on_ref, meta, a_ref, 0, base_row, rows)
    for copy in setup:
        copy.wait()
    place_windows(pupil_far, off_far, on_far, meta, a_ref, points, base_row, rows)

    def stage(it, which, h):
        along = h if which != 1 else 1 - h
        n, me, name = count[along], mine[along], axes[along]
        copies = []
        for d in offsets_far_first(n):
            peer = lax.rem(me + d, n)
            if which == 0:
                src, dst = part.at[it, h, peer], got1.at[it, h, me]
            elif which == 1:
                src, dst = sum1.at[it, h], got2.at[it, h, me]
            else:
                src, dst = sum2.at[it, h], img.at[it, h, me]
            slot = (which * 2 + h) * n
            copies.append(
                (remote(src, dst, st_send.at[it, slot + peer], st_recv.at[it, slot + me], {name: peer}), d)
            )
        for copy, d in copies:
            copy.start()
        return copies

    def arrive(it, which, h, copies):
        along = h if which != 1 else 1 - h
        n, me, name = count[along], mine[along], axes[along]
        into = (got1, got2, img)[which]
        for d in offsets_far_first(n):
            peer = lax.rem(me + d, n)
            slot = (which * 2 + h) * n
            remote(
                into.at[it, h, peer], into.at[it, h, peer], st_send.at[it, slot + peer],
                st_recv.at[it, slot + peer], {name: peer},
            ).wait_recv()
        pending.extend(copy for copy, d in copies)

    pending = []
    eye_low = None
    for it in range(ITERS):
        last = it == ITERS - 1
        left_own = omega_ref[...] if it == 0 else cpl_own[it]
        if it > 0:
            remote(cpl_own.at[it], cpl_far.at[it], c_send.at[it], c_recv.at[it], other).wait_recv()
        left_far = cpl_far[it]
        flights = []
        width = min(256, half)
        for h in range(2):
            for j in range(half // width):
                cols = slice(h * half + j * width, h * half + (j + 1) * width)
                total = dot_nn(left_own, a_ref[0:points, cols]) + dot_nn(
                    left_far, a_ref[points : 2 * points, cols]
                )
                part[it, h, :, :, j * width : (j + 1) * width] = total.reshape(
                    count[h], size // count[h], width
                )
            flights.append(stage(it, 0, h))
        second = []
        for h in range(2):
            me, n = mine[h], count[h]
            got1[it, h, me] = part[it, h, me]
            arrive(it, 0, h, flights[h])
            total = got1[it, h, 0]
            for p in range(1, n):
                total = total + got1[it, h, p]
            sum1[it, h] = total
            second.append(stage(it, 1, h))
            got2[it, h, mine[1 - h]] = total
        third = []
        for h in range(2):
            n = count[1 - h]
            arrive(it, 1, h, second[h])
            total = got2[it, h, 0]
            for p in range(1, n):
                total = total + got2[it, h, p]
            sum2[it, h] = total
            third.append(stage(it, 2, h))
            img[it, h, mine[h]] = total
        for h in range(2):
            arrive(it, 2, h, third[h])
            high, low = split2(img[it, h].reshape(size, half))
            split[0:size, h * half : (h + 1) * half] = high
            split[size : 2 * size, h * half : (h + 1) * half] = low
        if last:
            final = remote(img.at[it], img.at[it + 1], f_send.at[0], f_recv.at[0], other)
            final.start()
        both = split[...]
        square = dot_nt(both, both)
        square = square[:size] + square[size:]
        square = square + pltpu.roll(square, size, 1)
        lane = lax.broadcasted_iota(jnp.int32, (size // 2, LANES), 1)
        packed = jnp.where(lane < size, square[: size // 2], square[size // 2 :])
        gram_out[it] = packed
        my_slot = my_x * n_c + my_c
        gram_in[it, my_slot] = packed
        for i, (dx, dc) in enumerate(group):
            peer_x, peer_c = group_peer(dx, dc)
            copy = remote(
                gram_out.at[it], gram_in.at[it, my_slot], gram_send.at[it, i],
                gram_recv.at[it, my_slot], {"freq": peer_x, "src_2": peer_c},
            )
            copy.start()
            pending.append(copy)
        if not last:
            far = dot_nt(both, a_ref[points : 2 * points, :])
            w_far[it] = far[:size] + far[size:]
            swap = remote(w_far.at[it], w_far_in.at[it], w_send.at[it], w_recv.at[it], other)
            swap.start()
            pending.append(swap)
            own = dot_nt(both, a_ref[0:points, :])
            own = own[:size] + own[size:]
            swap.wait_recv()
            own = own + w_far_in[it]
            w_own[it] = own
            w_in[it, my_x] = own
            for d in offsets_far_first(n_x):
                peer = lax.rem(my_x + d, n_x)
                copy = remote(
                    w_own.at[it], w_in.at[it, my_x], x_send.at[it, d], x_recv.at[it, my_x],
                    {"freq": peer},
                )
                copy.start()
                pending.append(copy)
        for dx, dc in group:
            peer_x, peer_c = group_peer(dx, dc)
            slot = peer_x * n_c + peer_c
            remote(
                gram_out.at[it], gram_in.at[it, slot], gram_send.at[it, 0], gram_recv.at[it, slot],
                {"freq": peer_x, "src_2": peer_c},
            ).wait_recv()
        total = gram_in[it, 0]
        for p in range(1, n_x * n_c):
            total = total + gram_in[it, p]
        inv_high, inv_low = split2(inverse_factor(total * (1.0 / (G * G)), size))
        if not last:
            for d in offsets_far_first(n_x):
                peer = lax.rem(my_x + d, n_x)
                remote(
                    w_own.at[it], w_in.at[it, peer], x_send.at[it, d], x_recv.at[it, peer],
                    {"freq": peer},
                ).wait_recv()
            total = w_in[it, 0]
            for p in range(1, n_x):
                total = total + w_in[it, p]
            cpl_own[it + 1] = apply_factor(inv_high, inv_low, total).astype(jnp.bfloat16)
            copy = remote(
                cpl_own.at[it + 1], cpl_far.at[it + 1], c_send.at[it + 1], c_recv.at[it + 1], other
            )
            copy.start()
            pending.append(copy)
        else:
            final.wait()
            width = min(256, half)
            for c in range(2):
                slot = it + jnp.where(my_c == c, 0, 1)
                for h in range(2):
                    for j in range(half // width):
                        value = img[slot, h, :, :, j * width : (j + 1) * width].reshape(size, width)
                        start = (c * 2 + h) * half + j * width
                        out_ref[:, start : start + width] = apply_factor(inv_high, inv_low, value)
    for copy in pending:
        copy.wait_send()


def shards(pupil_block, source_on, offsets, omega):
    points = pupil_block.shape[0]
    size = omega.shape[1]
    n_y, n_z, n_c = (lax.axis_size(name) for name in SRC)
    n_x = lax.axis_size("freq")
    rows = G // (n_x * n_c)
    freqs = rows * G
    half = freqs // 2
    ky, kz = size // n_y, size // n_z
    assert n_y == n_z and n_c == 2
    f32, bf16, i32 = jnp.float32, jnp.bfloat16, jnp.int32
    vmem = pltpu.VMEM
    dma = pltpu.SemaphoreType.DMA
    scratch = [
        vmem((points, PB * PB), bf16), vmem((1, points), i32), vmem((2, points), i32),
        vmem((3, points, LANES), i32),
        vmem((2 * points, freqs), bf16),
        vmem((ITERS, size, points), bf16), vmem((ITERS, size, points), bf16),
        vmem((ITERS, 2, n_y, ky, half), f32), vmem((ITERS, 2, n_y, ky, half), f32),
        vmem((ITERS, 2, ky, half), f32), vmem((ITERS, 2, n_z, ky, half), f32),
        vmem((ITERS, 2, ky, half), f32), vmem((ITERS + 1, 2, n_y, ky, half), f32),
        vmem((2 * size, freqs), bf16),
        vmem((ITERS, size // 2, LANES), f32), vmem((ITERS, n_x * n_c, size // 2, LANES), f32),
        vmem((ITERS, size, points), f32), vmem((ITERS, size, points), f32),
        vmem((ITERS, size, points), f32), vmem((ITERS, n_x, size, points), f32),
        dma((4,)), dma((4,)), dma((ITERS, 6 * n_y)), dma((ITERS, 6 * n_y)),
        dma((ITERS, n_x * n_c)), dma((ITERS, n_x * n_c)), dma((ITERS,)), dma((ITERS,)),
        dma((ITERS, n_x)), dma((ITERS, n_x)), dma((ITERS,)), dma((ITERS,)), dma((1,)), dma((1,)),
    ]
    out = pl.pallas_call(
        functools.partial(kernel, (n_y, n_z, n_c, n_x)),
        out_shape=jax.ShapeDtypeStruct((size, freqs * n_c), f32),
        in_specs=[pl.BlockSpec(memory_space=pltpu.VMEM)] * 4,
        out_specs=pl.BlockSpec(memory_space=pltpu.VMEM),
        scratch_shapes=scratch,
        compiler_params=pltpu.CompilerParams(
            collective_id=0, has_side_effects=True, vmem_limit_bytes=60 * 1024 * 1024
        ),
    )(pupil_block, source_on.reshape(1, points), offsets, omega.T)
    return out.T


def solution(mesh):
    split = Mesh(
        mesh.devices.reshape(8, 8, 2, mesh.shape["freq"]), ("src_0", "src_1", "src_2", "freq")
    )
    return jax.shard_map(
        shards,
        mesh=split,
        in_specs=(P(SRC, None), P(SRC), P(None, SRC), P(SRC, None)),
        out_specs=P("freq", None),
        check_vma=False,
    )
```

```python
import functools

import jax
import jax.numpy as jnp
from jax import lax
from jax.experimental import pallas as pl
from jax.experimental.pallas import tpu as pltpu
from jax.sharding import Mesh
from jax.sharding import PartitionSpec as P

G = 128
PB = 32
ITERS = 3
LANES = 128
LEVELS = 32700.0
TINY = 1e-30
SRC = ("src_0", "src_1", "src_2")
MESH_ID = pl.DeviceIdType.MESH


def split2(value):
    high = value.astype(jnp.bfloat16)
    low = (value - high.astype(jnp.float32)).astype(jnp.bfloat16)
    return high, low


def dot_nn(left, right):
    return lax.dot_general(
        left, right, (((1,), (0,)), ((), ())), preferred_element_type=jnp.float32
    )


def dot_nt(left, right):
    return lax.dot_general(
        left, right, (((1,), (1,)), ((), ())), preferred_element_type=jnp.float32
    )


def apply_factor(inv_high, inv_low, high, low):
    return dot_nn(inv_high, high) + (dot_nn(inv_high, low) + dot_nn(inv_low, high))


def encode(value):
    top = jnp.maximum(jnp.max(jnp.abs(value), axis=1, keepdims=True), TINY)
    level = lax.round(value * (LEVELS / top), lax.RoundingMethod.TO_NEAREST_EVEN)
    return level.astype(jnp.int32), top


def diagonal(rows):
    shape = (rows, LANES)
    return lax.broadcasted_iota(jnp.int32, shape, 1) == lax.broadcasted_iota(jnp.int32, shape, 0)


def column_to_line(top):
    rows = top.shape[0]
    wide = jnp.broadcast_to(top, (rows, LANES))
    return jnp.sum(jnp.where(diagonal(rows), wide, 0.0), axis=0, keepdims=True)


def decode(level, line):
    rows = level.shape[0]
    wide = jnp.broadcast_to(line, (rows, LANES))
    top = jnp.sum(jnp.where(diagonal(rows), wide, 0.0), axis=1, keepdims=True)
    return level.astype(jnp.int32).astype(jnp.float32) * (top * (1.0 / LEVELS))


def place_windows(pupil_ref, off_ref, on_ref, meta_ref, a_ref, a_row, base_row, rows):
    points = pupil_ref.shape[0]
    per = LANES // PB
    chunk = min(64, points)

    def spread(line):
        return jnp.transpose(jnp.broadcast_to(line, (LANES, points)))

    meta_ref[0] = spread(off_ref[0:1, :])
    meta_ref[1] = spread(off_ref[1:2, :])
    meta_ref[2] = spread(on_ref[0:1, :])

    def block(index, carry):
        s0 = pl.multiple_of(index * chunk, chunk)
        row_off = meta_ref[0, pl.ds(s0, chunk), :]
        col_off = meta_ref[1, pl.ds(s0, chunk), :]
        lit = meta_ref[2, pl.ds(s0, chunk), :].astype(jnp.float32)
        lane = lax.broadcasted_iota(jnp.int32, (chunk, LANES), 1)
        shift = jnp.clip(base_row - row_off, -rows, PB) + rows
        window = pupil_ref[pl.ds(s0, chunk), :].astype(jnp.float32)
        tiles = [None] * (rows // per)
        tiles += [window[:, i * LANES : (i + 1) * LANES] * lit for i in range(PB // per)]
        tiles += [None] * (rows // per)
        zero = jnp.zeros((chunk, LANES), jnp.float32)

        def pick(mask, taken, kept):
            if taken is None and kept is None:
                return None
            return jnp.where(mask, zero if taken is None else taken, zero if kept is None else kept)

        kept_tiles = rows // per + 1
        for bit in reversed(range(((rows + PB) // per).bit_length())):
            step = 1 << bit
            mask = (shift & (step * per)) != 0
            count = kept_tiles + step - 1
            at = lambda i: tiles[i] if i < len(tiles) else None
            tiles = [pick(mask, at(i + step), at(i)) for i in range(count)]
        for step in (2, 1):
            mask = (shift & step) != 0
            turned = [None if t is None else pltpu.roll(t, LANES - PB * step, 1) for t in tiles]
            turned.append(None)
            inside = lane < LANES - PB * step
            moved = [pick(inside, turned[i], turned[i + 1]) for i in range(len(tiles))]
            tiles = [pick(mask, moved[i], tiles[i]) for i in range(len(tiles))]
        tiles = tiles[: rows // per]
        for bit in range(LANES.bit_length() - 1):
            mask = (col_off & (1 << bit)) != 0
            tiles = [jnp.where(mask, pltpu.roll(t, 1 << bit, 1), t) for t in tiles]
        inner = lane - col_off
        covered = (inner >= 0) & (inner < PB)
        for row in range(rows):
            tile, group = tiles[row // per], row % per
            if group:
                tile = pltpu.roll(tile, LANES - PB * group, 1)
            a_ref[pl.ds(a_row + s0, chunk), row * LANES : (row + 1) * LANES] = jnp.where(
                covered, tile, 0.0
            ).astype(jnp.bfloat16)
        return carry

    lax.fori_loop(0, points // chunk, block, 0)


def inverse_factor(packed, size):
    whole = jnp.concatenate([pltpu.roll(packed, size, 1), packed], axis=0)
    full = (8, LANES)
    lane = lax.broadcasted_iota(jnp.int32, full, 1)
    sub = lax.broadcasted_iota(jnp.int32, full, 0)
    tiles = []
    for t in range(size // 8):
        eye = jnp.where(lane == sub + 8 * t, 1.0, 0.0)
        tiles.append(jnp.where(lane < size, eye, whole[8 * t : 8 * t + 8]))
    wide = 4
    for k in range(0, size, wide):
        home, first = k // 8, k % 8
        columns = [
            [jnp.broadcast_to(tiles[t][:, size + k + j : size + k + j + 1], full) for j in range(wide)]
            for t in range(home, size // 8)
        ]
        lines = [jnp.broadcast_to(tiles[home][first + i : first + i + 1, :], full) for i in range(wide)]
        block = [
            [jnp.broadcast_to(columns[0][j][first + i : first + i + 1, :], full) for j in range(i + 1)]
            for i in range(wide)
        ]
        ratio, scaled = {}, []
        for p in range(wide):
            inverse = 1.0 / block[p][p]
            for i in range(p + 1, wide):
                ratio[i, p] = block[i][p] * inverse
                for j in range(p + 1, i + 1):
                    block[i][j] = block[i][j] - ratio[i, p] * block[j][p]
            for i in range(p + 1, wide):
                lines[i] = lines[i] - ratio[i, p] * lines[p]
            scaled.append(lines[p] * inverse)
        for t in range(home, size // 8):
            own = columns[t - home]
            taken = None
            for p in range(wide):
                weight = own[p]
                for q in range(p):
                    weight = weight - ratio[p, q] * own[q]
                own[p] = weight
                term = weight * scaled[p]
                taken = term if taken is None else taken + term
            updated = tiles[t] - taken
            if t == home:
                updated = jnp.where(sub >= first + wide, updated, tiles[t])
                for i in range(1, wide):
                    updated = jnp.where(sub == first + i, lines[i], updated)
            tiles[t] = updated
    done = []
    for t in range(size // 8):
        pivot = jnp.sum(jnp.where(lane == sub + (8 * t + size), tiles[t], 0.0), axis=1, keepdims=True)
        done.append(tiles[t] * lax.rsqrt(pivot))
    return jnp.concatenate(done, axis=0)[:, :size]


def kernel(
    sizes, pupil_ref, on_ref, off_ref, omega_ref, out_ref,
    pupil_far, on_far, off_far, meta, a_ref, cpl_own, cpl_far,
    level, level_top, part_q, part_s, got1_q, got1_s, sum1_q, sum1_s, got2_q, got2_s, sum2_q, sum2_s,
    img_q, img_s, split, gram_out, gram_in, w_far, w_far_in, w_own, w_in,
    setup_send, setup_recv, st_send, st_recv, gram_send, gram_recv, w_send, w_recv, x_send, x_recv,
    c_send, c_recv, f_send, f_recv,
):
    n_y, n_z, n_c, n_x = sizes
    my_y, my_z = lax.axis_index("src_0"), lax.axis_index("src_1")
    my_c, my_x = lax.axis_index("src_2"), lax.axis_index("freq")
    other = {"src_2": 1 - my_c}
    rows = G // (n_x * n_c)
    size = omega_ref.shape[0]
    points = pupil_ref.shape[0]
    half = rows * G // 2
    quarter = half // 2
    axes = ("src_0", "src_1")
    count = (n_y, n_z)
    mine = (my_y, my_z)
    kept = size // n_y

    def offsets_far_first(n):
        return sorted(range(1, n), key=lambda d: (-min(d, n - d), d))

    group = [(dx, dc) for dx in range(n_x) for dc in range(n_c) if dx or dc]

    def group_peer(dx, dc):
        peer_x = lax.rem(my_x + dx, n_x)
        peer_c = lax.rem(my_c + dc, n_c)
        return peer_x, peer_c

    barrier = pltpu.get_barrier_semaphore()
    for a in range(2):
        for d in range(1, count[a]):
            pl.semaphore_signal(
                barrier, inc=1, device_id={axes[a]: lax.rem(mine[a] + d, count[a])},
                device_id_type=MESH_ID,
            )
    for dx, dc in group:
        peer_x, peer_c = group_peer(dx, dc)
        pl.semaphore_signal(
            barrier, inc=1, device_id={"freq": peer_x, "src_2": peer_c}, device_id_type=MESH_ID
        )
    pl.semaphore_wait(barrier, n_y - 1 + n_z - 1 + len(group))

    def remote(src, dst, send, recv, device):
        return pltpu.make_async_remote_copy(
            src_ref=src, dst_ref=dst, send_sem=send, recv_sem=recv,
            device_id=device, device_id_type=MESH_ID,
        )

    setup = [
        remote(src, dst, setup_send.at[i], setup_recv.at[i], other)
        for i, (src, dst) in enumerate(
            ((off_ref, off_far), (on_ref, on_far), (omega_ref, cpl_far.at[0]), (pupil_ref, pupil_far))
        )
    ]
    for copy in setup:
        copy.start()
    base_row = my_x * (rows * n_c) + my_c * rows
    place_windows(pupil_ref, off_ref, on_ref, meta, a_ref, 0, base_row, rows)
    for copy in setup:
        copy.wait()
    place_windows(pupil_far, off_far, on_far, meta, a_ref, points, base_row, rows)

    outgoing = ((part_q, part_s), (sum1_q, sum1_s), (sum2_q, sum2_s))
    incoming = ((got1_q, got1_s), (got2_q, got2_s), (img_q, img_s))

    def ring(which, h):
        along = h if which != 1 else 1 - h
        return count[along], mine[along], axes[along]

    def stage(it, which, h):
        n, me, name = ring(which, h)
        for d in offsets_far_first(n):
            peer = lax.rem(me + d, n)
            slot = (which * 2 + h) * n
            for i in range(2):
                src = outgoing[which][i].at[it, h]
                copy = remote(
                    src.at[peer] if which == 0 else src, incoming[which][i].at[it, h, me],
                    st_send.at[it, i, slot + peer], st_recv.at[it, i, slot + me], {name: peer},
                )
                copy.start()
                pending.append(copy)
        for i in range(2):
            src = outgoing[which][i].at[it, h]
            incoming[which][i][it, h, me] = src[me] if which == 0 else src[...]

    def arrive(it, which, h):
        n, me, name = ring(which, h)
        for d in offsets_far_first(n):
            peer = lax.rem(me + d, n)
            slot = (which * 2 + h) * n
            for i in range(2):
                into = incoming[which][i].at[it, h, peer]
                remote(
                    into, into, st_send.at[it, i, slot + peer], st_recv.at[it, i, slot + peer],
                    {name: peer},
                ).wait_recv()

    def total_of(it, which, h):
        n = ring(which, h)[0]
        levels, lines = incoming[which]
        total = decode(levels[it, h, 0], lines[it, h, 0])
        for p in range(1, n):
            total = total + decode(levels[it, h, p], lines[it, h, p])
        value, top = encode(total)
        levels, lines = outgoing[which + 1]
        levels[it, h] = value.astype(jnp.int16)
        lines[it, h] = column_to_line(top)

    def split_images(slot, h, to):
        together = max(1, 16 // kept)
        for g in range(0, n_y, together):
            values = [decode(img_q[slot, h, g + i], img_s[slot, h, g + i]) for i in range(together)]
            for b in range(2):
                part = [v[b * kept : (b + 1) * kept] for v in values]
                high, low = split2(jnp.concatenate(part, axis=0) if together > 1 else part[0])
                cols = slice(h * half + b * quarter, h * half + (b + 1) * quarter)
                split[to, g * kept : (g + together) * kept, cols] = high
                split[to, size + g * kept : size + (g + together) * kept, cols] = low

    pending = []
    for it in range(ITERS):
        last = it == ITERS - 1
        left_own = omega_ref[...] if it == 0 else cpl_own[it]
        if it > 0:
            remote(cpl_own.at[it], cpl_far.at[it], c_send.at[it], c_recv.at[it], other).wait_recv()
        left_far = cpl_far[it]
        for h in range(2):
            for b in range(2):
                cols = slice(h * half + b * quarter, h * half + (b + 1) * quarter)
                total = dot_nn(left_own, a_ref[0:points, cols]) + dot_nn(
                    left_far, a_ref[points : 2 * points, cols]
                )
                value, top = encode(total)
                level[:, b * kept : (b + 1) * kept, :] = value.reshape(n_y, kept, quarter)
                level_top[:, b * kept : (b + 1) * kept, :] = jnp.broadcast_to(
                    top, (size, LANES)
                ).reshape(n_y, kept, LANES)
            for g in range(n_y):
                part_q[it, h, g] = level[g].astype(jnp.int16)
                part_s[it, h, g] = column_to_line(level_top[g][:, 0:1])
            stage(it, 0, h)
        for h in range(2):
            arrive(it, 0, h)
            total_of(it, 0, h)
            stage(it, 1, h)
        for h in range(2):
            arrive(it, 1, h)
            total_of(it, 1, h)
            stage(it, 2, h)
        for h in range(2):
            arrive(it, 2, h)
            split_images(it, h, 0)
        if last:
            final = [
                remote(img_q.at[it], img_q.at[it + 1], f_send.at[0], f_recv.at[0], other),
                remote(img_s.at[it], img_s.at[it + 1], f_send.at[1], f_recv.at[1], other),
            ]
            for copy in final:
                copy.start()
        both = split[0]
        square = dot_nt(both, both)
        square = square[:size] + square[size:]
        square = square + pltpu.roll(square, size, 1)
        lane = lax.broadcasted_iota(jnp.int32, (size // 2, LANES), 1)
        packed = jnp.where(lane < size, square[: size // 2], square[size // 2 :])
        gram_out[it] = packed
        my_slot = my_x * n_c + my_c
        gram_in[it, my_slot] = packed
        for i, (dx, dc) in enumerate(group):
            peer_x, peer_c = group_peer(dx, dc)
            copy = remote(
                gram_out.at[it], gram_in.at[it, my_slot], gram_send.at[it, i],
                gram_recv.at[it, my_slot], {"freq": peer_x, "src_2": peer_c},
            )
            copy.start()
            pending.append(copy)
        if not last:
            far = dot_nt(both, a_ref[points : 2 * points, :])
            w_far[it] = far[:size] + far[size:]
            swap = remote(w_far.at[it], w_far_in.at[it], w_send.at[it], w_recv.at[it], other)
            swap.start()
            pending.append(swap)
            own = dot_nt(both, a_ref[0:points, :])
            own = own[:size] + own[size:]
            swap.wait_recv()
            own = own + w_far_in[it]
            w_own[it] = own
            w_in[it, my_x] = own
            for d in offsets_far_first(n_x):
                peer = lax.rem(my_x + d, n_x)
                copy = remote(
                    w_own.at[it], w_in.at[it, my_x], x_send.at[it, d], x_recv.at[it, my_x],
                    {"freq": peer},
                )
                copy.start()
                pending.append(copy)
        else:
            for copy in final:
                copy.wait_recv()
            pending.extend(final)
            for h in range(2):
                split_images(it + 1, h, 1)
        for dx, dc in group:
            peer_x, peer_c = group_peer(dx, dc)
            slot = peer_x * n_c + peer_c
            remote(
                gram_out.at[it], gram_in.at[it, slot], gram_send.at[it, 0], gram_recv.at[it, slot],
                {"freq": peer_x, "src_2": peer_c},
            ).wait_recv()
        total = gram_in[it, 0]
        for p in range(1, n_x * n_c):
            total = total + gram_in[it, p]
        inv_high, inv_low = split2(inverse_factor(total * (1.0 / (G * G)), size))
        if not last:
            for d in offsets_far_first(n_x):
                peer = lax.rem(my_x + d, n_x)
                remote(
                    w_own.at[it], w_in.at[it, peer], x_send.at[it, d], x_recv.at[it, peer],
                    {"freq": peer},
                ).wait_recv()
            total = w_in[it, 0]
            for p in range(1, n_x):
                total = total + w_in[it, p]
            high, low = split2(total)
            cpl_own[it + 1] = apply_factor(inv_high, inv_low, high, low).astype(jnp.bfloat16)
            copy = remote(
                cpl_own.at[it + 1], cpl_far.at[it + 1], c_send.at[it + 1], c_recv.at[it + 1], other
            )
            copy.start()
            pending.append(copy)
        else:
            width = min(256, half)
            for c in range(2):
                slot = jnp.where(my_c == c, 0, 1)
                for j in range(2 * half // width):
                    cols = slice(j * width, (j + 1) * width)
                    start = c * 2 * half + j * width
                    out_ref[:, start : start + width] = apply_factor(
                        inv_high, inv_low, split[slot, 0:size, cols], split[slot, size : 2 * size, cols]
                    )
    for copy in pending:
        copy.wait_send()


def shards(pupil_block, source_on, offsets, omega):
    points = pupil_block.shape[0]
    size = omega.shape[1]
    n_y, n_z, n_c = (lax.axis_size(name) for name in SRC)
    n_x = lax.axis_size("freq")
    rows = G // (n_x * n_c)
    freqs = rows * G
    assert n_y == n_z and n_c == 2
    tall, quarter = 2 * (size // n_y), freqs // 4
    f32, bf16, i32, i16 = jnp.float32, jnp.bfloat16, jnp.int32, jnp.int16
    vmem = pltpu.VMEM
    dma = pltpu.SemaphoreType.DMA

    def blocks(*lead):
        return [vmem((*lead, tall, quarter), i16), vmem((*lead, 1, LANES), f32)]

    scratch = [
        vmem((points, PB * PB), bf16), vmem((1, points), i32), vmem((2, points), i32),
        vmem((3, points, LANES), i32),
        vmem((2 * points, freqs), bf16),
        vmem((ITERS, size, points), bf16), vmem((ITERS, size, points), bf16),
        vmem((n_y, tall, quarter), i32), vmem((n_y, tall, LANES), f32),
        *blocks(ITERS, 2, n_y), *blocks(ITERS, 2, n_y), *blocks(ITERS, 2), *blocks(ITERS, 2, n_z),
        *blocks(ITERS, 2), *blocks(ITERS + 1, 2, n_y),
        vmem((2, 2 * size, freqs), bf16),
        vmem((ITERS, size // 2, LANES), f32), vmem((ITERS, n_x * n_c, size // 2, LANES), f32),
        vmem((ITERS, size, points), f32), vmem((ITERS, size, points), f32),
        vmem((ITERS, size, points), f32), vmem((ITERS, n_x, size, points), f32),
        dma((4,)), dma((4,)), dma((ITERS, 2, 6 * n_y)), dma((ITERS, 2, 6 * n_y)),
        dma((ITERS, n_x * n_c)), dma((ITERS, n_x * n_c)), dma((ITERS,)), dma((ITERS,)),
        dma((ITERS, n_x)), dma((ITERS, n_x)), dma((ITERS,)), dma((ITERS,)), dma((2,)), dma((2,)),
    ]
    out = pl.pallas_call(
        functools.partial(kernel, (n_y, n_z, n_c, n_x)),
        out_shape=jax.ShapeDtypeStruct((size, freqs * n_c), f32),
        in_specs=[pl.BlockSpec(memory_space=pltpu.VMEM)] * 4,
        out_specs=pl.BlockSpec(memory_space=pltpu.VMEM),
        scratch_shapes=scratch,
        compiler_params=pltpu.CompilerParams(
            collective_id=0, has_side_effects=True, vmem_limit_bytes=60 * 1024 * 1024
        ),
    )(pupil_block, source_on.reshape(1, points), offsets, omega.T)
    return out.T


def solution(mesh):
    split = Mesh(
        mesh.devices.reshape(8, 8, 2, mesh.shape["freq"]), ("src_0", "src_1", "src_2", "freq")
    )
    return jax.shard_map(
        shards,
        mesh=split,
        in_specs=(P(SRC, None), P(SRC), P(None, SRC), P(SRC, None)),
        out_specs=P("freq", None),
        check_vma=False,
    )
```

```python
import functools

import jax
import jax.numpy as jnp
from jax import lax
from jax.experimental import pallas as pl
from jax.experimental.pallas import tpu as pltpu
from jax.sharding import Mesh
from jax.sharding import PartitionSpec as P

G = 128
PB = 32
ITERS = 3
LANES = 128
LEVELS = 32700.0
TINY = 1e-30
SRC = ("src_0", "src_1", "src_2")
MESH_ID = pl.DeviceIdType.MESH


def split2(value):
    high = value.astype(jnp.bfloat16)
    low = (value - high.astype(jnp.float32)).astype(jnp.bfloat16)
    return high, low


def dot_nn(left, right):
    return lax.dot_general(
        left, right, (((1,), (0,)), ((), ())), preferred_element_type=jnp.float32
    )


def dot_nt(left, right):
    return lax.dot_general(
        left, right, (((1,), (1,)), ((), ())), preferred_element_type=jnp.float32
    )


def apply_factor(inv_high, inv_low, high, low):
    return dot_nn(inv_high, high) + (dot_nn(inv_high, low) + dot_nn(inv_low, high))


def encode(value):
    top = jnp.maximum(jnp.max(jnp.abs(value), axis=1, keepdims=True), TINY)
    level = lax.round(value * (LEVELS / top), lax.RoundingMethod.TO_NEAREST_EVEN)
    return level.astype(jnp.int32), top


def diagonal(rows):
    shape = (rows, LANES)
    return lax.broadcasted_iota(jnp.int32, shape, 1) == lax.broadcasted_iota(jnp.int32, shape, 0)


def column_to_line(top):
    rows = top.shape[0]
    wide = jnp.broadcast_to(top, (rows, LANES))
    return jnp.sum(jnp.where(diagonal(rows), wide, 0.0), axis=0, keepdims=True)


def decode(level, line):
    rows = level.shape[0]
    wide = jnp.broadcast_to(line, (rows, LANES))
    top = jnp.sum(jnp.where(diagonal(rows), wide, 0.0), axis=1, keepdims=True)
    return level.astype(jnp.int32).astype(jnp.float32) * (top * (1.0 / LEVELS))


def place_windows(pupil_ref, off_ref, on_ref, meta_ref, a_ref, a_row, base_row, rows):
    points = pupil_ref.shape[0]
    per = LANES // PB
    chunk = min(64, points)

    def spread(line):
        return jnp.transpose(jnp.broadcast_to(line, (LANES, points)))

    meta_ref[0] = spread(off_ref[0:1, :])
    meta_ref[1] = spread(off_ref[1:2, :])
    meta_ref[2] = spread(on_ref[0:1, :])

    def block(index, carry):
        s0 = pl.multiple_of(index * chunk, chunk)
        row_off = meta_ref[0, pl.ds(s0, chunk), :]
        col_off = meta_ref[1, pl.ds(s0, chunk), :]
        lit = meta_ref[2, pl.ds(s0, chunk), :].astype(jnp.float32)
        lane = lax.broadcasted_iota(jnp.int32, (chunk, LANES), 1)
        shift = jnp.clip(base_row - row_off, -rows, PB) + rows
        window = pupil_ref[pl.ds(s0, chunk), :].astype(jnp.float32)
        tiles = [None] * (rows // per)
        tiles += [window[:, i * LANES : (i + 1) * LANES] * lit for i in range(PB // per)]
        tiles += [None] * (rows // per)
        zero = jnp.zeros((chunk, LANES), jnp.float32)

        def pick(mask, taken, kept):
            if taken is None and kept is None:
                return None
            return jnp.where(mask, zero if taken is None else taken, zero if kept is None else kept)

        kept_tiles = rows // per + 1
        for bit in reversed(range(((rows + PB) // per).bit_length())):
            step = 1 << bit
            mask = (shift & (step * per)) != 0
            count = kept_tiles + step - 1
            at = lambda i: tiles[i] if i < len(tiles) else None
            tiles = [pick(mask, at(i + step), at(i)) for i in range(count)]
        for step in (2, 1):
            mask = (shift & step) != 0
            turned = [None if t is None else pltpu.roll(t, LANES - PB * step, 1) for t in tiles]
            turned.append(None)
            inside = lane < LANES - PB * step
            moved = [pick(inside, turned[i], turned[i + 1]) for i in range(len(tiles))]
            tiles = [pick(mask, moved[i], tiles[i]) for i in range(len(tiles))]
        tiles = tiles[: rows // per]
        for bit in range(LANES.bit_length() - 1):
            mask = (col_off & (1 << bit)) != 0
            tiles = [jnp.where(mask, pltpu.roll(t, 1 << bit, 1), t) for t in tiles]
        inner = lane - col_off
        covered = (inner >= 0) & (inner < PB)
        for row in range(rows):
            tile, group = tiles[row // per], row % per
            if group:
                tile = pltpu.roll(tile, LANES - PB * group, 1)
            a_ref[pl.ds(a_row + s0, chunk), row * LANES : (row + 1) * LANES] = jnp.where(
                covered, tile, 0.0
            ).astype(jnp.bfloat16)
        return carry

    lax.fori_loop(0, points // chunk, block, 0)


def inverse_factor(packed, size):
    whole = jnp.concatenate([pltpu.roll(packed, size, 1), packed], axis=0)
    full = (8, LANES)
    lane = lax.broadcasted_iota(jnp.int32, full, 1)
    sub = lax.broadcasted_iota(jnp.int32, full, 0)
    tiles = []
    for t in range(size // 8):
        eye = jnp.where(lane == sub + 8 * t, 1.0, 0.0)
        tiles.append(jnp.where(lane < size, eye, whole[8 * t : 8 * t + 8]))
    wide = 4
    for k in range(0, size, wide):
        home, first = k // 8, k % 8
        columns = [
            [jnp.broadcast_to(tiles[t][:, size + k + j : size + k + j + 1], full) for j in range(wide)]
            for t in range(home, size // 8)
        ]
        lines = [jnp.broadcast_to(tiles[home][first + i : first + i + 1, :], full) for i in range(wide)]
        block = [
            [jnp.broadcast_to(columns[0][j][first + i : first + i + 1, :], full) for j in range(i + 1)]
            for i in range(wide)
        ]
        ratio, scaled = {}, []
        for p in range(wide):
            inverse = 1.0 / block[p][p]
            for i in range(p + 1, wide):
                ratio[i, p] = block[i][p] * inverse
                for j in range(p + 1, i + 1):
                    block[i][j] = block[i][j] - ratio[i, p] * block[j][p]
            for i in range(p + 1, wide):
                lines[i] = lines[i] - ratio[i, p] * lines[p]
            scaled.append(lines[p] * inverse)
        for t in range(home, size // 8):
            own = columns[t - home]
            taken = None
            for p in range(wide):
                weight = own[p]
                for q in range(p):
                    weight = weight - ratio[p, q] * own[q]
                own[p] = weight
                term = weight * scaled[p]
                taken = term if taken is None else taken + term
            updated = tiles[t] - taken
            if t == home:
                updated = jnp.where(sub >= first + wide, updated, tiles[t])
                for i in range(1, wide):
                    updated = jnp.where(sub == first + i, lines[i], updated)
            tiles[t] = updated
    done = []
    for t in range(size // 8):
        pivot = jnp.sum(jnp.where(lane == sub + (8 * t + size), tiles[t], 0.0), axis=1, keepdims=True)
        done.append(tiles[t] * lax.rsqrt(pivot))
    return jnp.concatenate(done, axis=0)[:, :size]


def kernel(
    sizes, pupil_hbm, on_hbm, off_hbm, omega_hbm, out_ref,
    pupil_ref, on_ref, off_ref, omega_ref, pupil_far, on_far, off_far, meta, a_ref, cpl_own, cpl_far,
    level, level_top, part_q, part_s, got1_q, got1_s, sum1_q, sum1_s, got2_q, got2_s, sum2_q, sum2_s,
    img_q, img_s, split, gram_out, gram_in, w_far, w_far_in, w_q, w_s, w_in_q, w_in_s,
    setup_send, setup_recv, st_send, st_recv, gram_send, gram_recv, w_send, w_recv, x_send, x_recv,
    c_send, c_recv, f_send, f_recv, load_sem,
):
    n_y, n_z, n_c, n_x = sizes
    my_y, my_z = lax.axis_index("src_0"), lax.axis_index("src_1")
    my_c, my_x = lax.axis_index("src_2"), lax.axis_index("freq")
    other = {"src_2": 1 - my_c}
    rows = G // (n_x * n_c)
    size = omega_hbm.shape[0]
    points = pupil_hbm.shape[0]
    half = rows * G // 2
    quarter = half // 2
    axes = ("src_0", "src_1")
    count = (n_y, n_z)
    mine = (my_y, my_z)
    kept = size // n_y

    def offsets_far_first(n):
        return sorted(range(1, n), key=lambda d: (-min(d, n - d), d))

    group = [(dx, dc) for dx in range(n_x) for dc in range(n_c) if dx or dc]

    def group_peer(dx, dc):
        peer_x = lax.rem(my_x + dx, n_x)
        peer_c = lax.rem(my_c + dc, n_c)
        return peer_x, peer_c

    barrier = pltpu.get_barrier_semaphore()
    for a in range(2):
        for d in range(1, count[a]):
            pl.semaphore_signal(
                barrier, inc=1, device_id={axes[a]: lax.rem(mine[a] + d, count[a])},
                device_id_type=MESH_ID,
            )
    for dx, dc in group:
        peer_x, peer_c = group_peer(dx, dc)
        pl.semaphore_signal(
            barrier, inc=1, device_id={"freq": peer_x, "src_2": peer_c}, device_id_type=MESH_ID
        )
    local = [
        pltpu.make_async_copy(src, dst, load_sem.at[i])
        for i, (src, dst) in enumerate(
            ((off_hbm, off_ref), (on_hbm, on_ref), (omega_hbm, omega_ref), (pupil_hbm, pupil_ref))
        )
    ]
    for copy in local:
        copy.start()
    pl.semaphore_wait(barrier, n_y - 1 + n_z - 1 + len(group))

    def remote(src, dst, send, recv, device):
        return pltpu.make_async_remote_copy(
            src_ref=src, dst_ref=dst, send_sem=send, recv_sem=recv,
            device_id=device, device_id_type=MESH_ID,
        )

    setup = [
        remote(src, dst, setup_send.at[i], setup_recv.at[i], other)
        for i, (src, dst) in enumerate(
            ((off_hbm, off_far), (on_hbm, on_far), (omega_hbm, cpl_far.at[0]), (pupil_hbm, pupil_far))
        )
    ]
    for copy in setup:
        copy.start()
    for copy in local:
        copy.wait()
    base_row = my_x * (rows * n_c) + my_c * rows
    place_windows(pupil_ref, off_ref, on_ref, meta, a_ref, 0, base_row, rows)
    for copy in setup:
        copy.wait()
    place_windows(pupil_far, off_far, on_far, meta, a_ref, points, base_row, rows)

    outgoing = ((part_q, part_s), (sum1_q, sum1_s), (sum2_q, sum2_s))
    incoming = ((got1_q, got1_s), (got2_q, got2_s), (img_q, img_s))

    def ring(which, h):
        along = h if which != 1 else 1 - h
        return count[along], mine[along], axes[along]

    def stage(it, which, h):
        n, me, name = ring(which, h)
        for d in offsets_far_first(n):
            peer = lax.rem(me + d, n)
            slot = (which * 2 + h) * n
            for i in range(2):
                src = outgoing[which][i].at[it, h]
                copy = remote(
                    src.at[peer] if which == 0 else src, incoming[which][i].at[it, h, me],
                    st_send.at[it, i, slot + peer], st_recv.at[it, i, slot + me], {name: peer},
                )
                copy.start()
                pending.append(copy)
        for i in range(2):
            src = outgoing[which][i].at[it, h]
            incoming[which][i][it, h, me] = src[me] if which == 0 else src[...]

    def arrive(it, which, h):
        n, me, name = ring(which, h)
        for d in offsets_far_first(n):
            peer = lax.rem(me + d, n)
            slot = (which * 2 + h) * n
            for i in range(2):
                into = incoming[which][i].at[it, h, peer]
                remote(
                    into, into, st_send.at[it, i, slot + peer], st_recv.at[it, i, slot + peer],
                    {name: peer},
                ).wait_recv()

    def total_of(it, which, h):
        n = ring(which, h)[0]
        levels, lines = incoming[which]
        total = decode(levels[it, h, 0], lines[it, h, 0])
        for p in range(1, n):
            total = total + decode(levels[it, h, p], lines[it, h, p])
        value, top = encode(total)
        levels, lines = outgoing[which + 1]
        levels[it, h] = value.astype(jnp.int16)
        lines[it, h] = column_to_line(top)

    def split_images(slot, h, to):
        together = max(1, 16 // kept)
        for g in range(0, n_y, together):
            values = [decode(img_q[slot, h, g + i], img_s[slot, h, g + i]) for i in range(together)]
            for b in range(2):
                part = [v[b * kept : (b + 1) * kept] for v in values]
                high, low = split2(jnp.concatenate(part, axis=0) if together > 1 else part[0])
                cols = slice(h * half + b * quarter, h * half + (b + 1) * quarter)
                split[to, g * kept : (g + together) * kept, cols] = high
                split[to, size + g * kept : size + (g + together) * kept, cols] = low

    pending = []
    for it in range(ITERS):
        last = it == ITERS - 1
        left_own = omega_ref[...] if it == 0 else cpl_own[it]
        if it > 0:
            remote(cpl_own.at[it], cpl_far.at[it], c_send.at[it], c_recv.at[it], other).wait_recv()
        left_far = cpl_far[it]
        for h in range(2):
            for b in range(2):
                cols = slice(h * half + b * quarter, h * half + (b + 1) * quarter)
                total = dot_nn(left_own, a_ref[0:points, cols]) + dot_nn(
                    left_far, a_ref[points : 2 * points, cols]
                )
                value, top = encode(total)
                level[:, b * kept : (b + 1) * kept, :] = value.reshape(n_y, kept, quarter)
                level_top[:, b * kept : (b + 1) * kept, :] = jnp.broadcast_to(
                    top, (size, LANES)
                ).reshape(n_y, kept, LANES)
            for g in range(n_y):
                part_q[it, h, g] = level[g].astype(jnp.int16)
                part_s[it, h, g] = column_to_line(level_top[g][:, 0:1])
            stage(it, 0, h)
        for h in range(2):
            arrive(it, 0, h)
            total_of(it, 0, h)
            stage(it, 1, h)
        for h in range(2):
            arrive(it, 1, h)
            total_of(it, 1, h)
            stage(it, 2, h)
        for h in range(2):
            arrive(it, 2, h)
            split_images(it, h, 0)
        if last:
            final = [
                remote(img_q.at[it], img_q.at[it + 1], f_send.at[0], f_recv.at[0], other),
                remote(img_s.at[it], img_s.at[it + 1], f_send.at[1], f_recv.at[1], other),
            ]
            for copy in final:
                copy.start()
        both = split[0]
        square = dot_nt(both, both)
        square = square[:size] + square[size:]
        square = square + pltpu.roll(square, size, 1)
        lane = lax.broadcasted_iota(jnp.int32, (size // 2, LANES), 1)
        packed = jnp.where(lane < size, square[: size // 2], square[size // 2 :])
        gram_out[it] = packed
        my_slot = my_x * n_c + my_c
        gram_in[it, my_slot] = packed
        for i, (dx, dc) in enumerate(group):
            peer_x, peer_c = group_peer(dx, dc)
            copy = remote(
                gram_out.at[it], gram_in.at[it, my_slot], gram_send.at[it, i],
                gram_recv.at[it, my_slot], {"freq": peer_x, "src_2": peer_c},
            )
            copy.start()
            pending.append(copy)
        if not last:
            far = dot_nt(both, a_ref[points : 2 * points, :])
            w_far[it] = far[:size] + far[size:]
            swap = remote(w_far.at[it], w_far_in.at[it], w_send.at[it], w_recv.at[it], other)
            swap.start()
            pending.append(swap)
            own = dot_nt(both, a_ref[0:points, :])
            own = own[:size] + own[size:]
            swap.wait_recv()
            own = own + w_far_in[it]
            value, top = encode(own)
            w_q[it] = value.astype(jnp.int16)
            w_s[it] = column_to_line(top)
            for d in offsets_far_first(n_x):
                peer = lax.rem(my_x + d, n_x)
                for i, (src, dst) in enumerate(((w_q, w_in_q), (w_s, w_in_s))):
                    copy = remote(
                        src.at[it], dst.at[it, my_x], x_send.at[it, i, d], x_recv.at[it, i, my_x],
                        {"freq": peer},
                    )
                    copy.start()
                    pending.append(copy)
            w_in_q[it, my_x] = w_q[it]
            w_in_s[it, my_x] = w_s[it]
        else:
            for copy in final:
                copy.wait_recv()
            pending.extend(final)
            for h in range(2):
                split_images(it + 1, h, 1)
        for dx, dc in group:
            peer_x, peer_c = group_peer(dx, dc)
            slot = peer_x * n_c + peer_c
            remote(
                gram_out.at[it], gram_in.at[it, slot], gram_send.at[it, 0], gram_recv.at[it, slot],
                {"freq": peer_x, "src_2": peer_c},
            ).wait_recv()
        total = gram_in[it, 0]
        for p in range(1, n_x * n_c):
            total = total + gram_in[it, p]
        inv_high, inv_low = split2(inverse_factor(total * (1.0 / (G * G)), size))
        if not last:
            for d in offsets_far_first(n_x):
                peer = lax.rem(my_x + d, n_x)
                for i, dst in enumerate((w_in_q, w_in_s)):
                    remote(
                        dst.at[it, peer], dst.at[it, peer], x_send.at[it, i, d],
                        x_recv.at[it, i, peer], {"freq": peer},
                    ).wait_recv()
            total = decode(w_in_q[it, 0], w_in_s[it, 0])
            for p in range(1, n_x):
                total = total + decode(w_in_q[it, p], w_in_s[it, p])
            high, low = split2(total)
            cpl_own[it + 1] = apply_factor(inv_high, inv_low, high, low).astype(jnp.bfloat16)
            copy = remote(
                cpl_own.at[it + 1], cpl_far.at[it + 1], c_send.at[it + 1], c_recv.at[it + 1], other
            )
            copy.start()
            pending.append(copy)
        else:
            width = min(256, half)
            for c in range(2):
                slot = jnp.where(my_c == c, 0, 1)
                for j in range(2 * half // width):
                    cols = slice(j * width, (j + 1) * width)
                    start = c * 2 * half + j * width
                    out_ref[:, start : start + width] = apply_factor(
                        inv_high, inv_low, split[slot, 0:size, cols], split[slot, size : 2 * size, cols]
                    )
    for copy in pending:
        copy.wait_send()


def shards(pupil_block, source_on, offsets, omega):
    points = pupil_block.shape[0]
    size = omega.shape[1]
    n_y, n_z, n_c = (lax.axis_size(name) for name in SRC)
    n_x = lax.axis_size("freq")
    rows = G // (n_x * n_c)
    freqs = rows * G
    assert n_y == n_z and n_c == 2
    tall, quarter = 2 * (size // n_y), freqs // 4
    f32, bf16, i32, i16 = jnp.float32, jnp.bfloat16, jnp.int32, jnp.int16
    vmem = pltpu.VMEM
    dma = pltpu.SemaphoreType.DMA

    def blocks(*lead):
        return [vmem((*lead, tall, quarter), i16), vmem((*lead, 1, LANES), f32)]

    scratch = [
        vmem((points, PB * PB), bf16), vmem((1, points), i32), vmem((2, points), i32),
        vmem((size, points), bf16),
        vmem((points, PB * PB), bf16), vmem((1, points), i32), vmem((2, points), i32),
        vmem((3, points, LANES), i32),
        vmem((2 * points, freqs), bf16),
        vmem((ITERS, size, points), bf16), vmem((ITERS, size, points), bf16),
        vmem((n_y, tall, quarter), i32), vmem((n_y, tall, LANES), f32),
        *blocks(ITERS, 2, n_y), *blocks(ITERS, 2, n_y), *blocks(ITERS, 2), *blocks(ITERS, 2, n_z),
        *blocks(ITERS, 2), *blocks(ITERS + 1, 2, n_y),
        vmem((2, 2 * size, freqs), bf16),
        vmem((ITERS, size // 2, LANES), f32), vmem((ITERS, n_x * n_c, size // 2, LANES), f32),
        vmem((ITERS, size, points), f32), vmem((ITERS, size, points), f32),
        vmem((ITERS, size, points), i16), vmem((ITERS, 1, LANES), f32),
        vmem((ITERS, n_x, size, points), i16), vmem((ITERS, n_x, 1, LANES), f32),
        dma((4,)), dma((4,)), dma((ITERS, 2, 6 * n_y)), dma((ITERS, 2, 6 * n_y)),
        dma((ITERS, n_x * n_c)), dma((ITERS, n_x * n_c)), dma((ITERS,)), dma((ITERS,)),
        dma((ITERS, 2, n_x)), dma((ITERS, 2, n_x)), dma((ITERS,)), dma((ITERS,)), dma((2,)), dma((2,)),
        dma((4,)),
    ]
    out = pl.pallas_call(
        functools.partial(kernel, (n_y, n_z, n_c, n_x)),
        out_shape=jax.ShapeDtypeStruct((size, freqs * n_c), f32),
        in_specs=[pl.BlockSpec(memory_space=pltpu.HBM)] * 4,
        out_specs=pl.BlockSpec(memory_space=pltpu.VMEM),
        scratch_shapes=scratch,
        compiler_params=pltpu.CompilerParams(
            collective_id=0, has_side_effects=True, vmem_limit_bytes=14 * 1024 * 1024
        ),
    )(pupil_block, source_on.reshape(1, points), offsets, omega.T)
    return out.T


def solution(mesh):
    split = Mesh(
        mesh.devices.reshape(8, 8, 2, mesh.shape["freq"]), ("src_0", "src_1", "src_2", "freq")
    )
    return jax.shard_map(
        shards,
        mesh=split,
        in_specs=(P(SRC, None), P(SRC), P(None, SRC), P(SRC, None)),
        out_specs=P("freq", None),
        check_vma=False,
    )
```

```python
import functools

import jax
import jax.numpy as jnp
from jax import lax
from jax.experimental import pallas as pl
from jax.experimental.pallas import tpu as pltpu
from jax.sharding import Mesh
from jax.sharding import PartitionSpec as P

G = 128
PB = 32
ITERS = 3
LANES = 128
LEVELS = 32700.0
TINY = 1e-30
SRC = ("src_0", "src_1", "src_2")
MESH_ID = pl.DeviceIdType.MESH


def split2(value):
    high = value.astype(jnp.bfloat16)
    low = (value - high.astype(jnp.float32)).astype(jnp.bfloat16)
    return high, low


def dot_nn(left, right):
    return lax.dot_general(
        left, right, (((1,), (0,)), ((), ())), preferred_element_type=jnp.float32
    )


def dot_nt(left, right):
    return lax.dot_general(
        left, right, (((1,), (1,)), ((), ())), preferred_element_type=jnp.float32
    )


def apply_factor(inv_high, inv_low, high, low):
    return dot_nn(inv_high, high) + (dot_nn(inv_high, low) + dot_nn(inv_low, high))


def encode(value):
    top = jnp.maximum(jnp.max(jnp.abs(value), axis=1, keepdims=True), TINY)
    level = lax.round(value * (LEVELS / top), lax.RoundingMethod.TO_NEAREST_EVEN)
    return level.astype(jnp.int32), top


def diagonal(rows):
    shape = (rows, LANES)
    return lax.broadcasted_iota(jnp.int32, shape, 1) == lax.broadcasted_iota(jnp.int32, shape, 0)


def column_to_line(top):
    rows = top.shape[0]
    wide = jnp.broadcast_to(top, (rows, LANES))
    return jnp.sum(jnp.where(diagonal(rows), wide, 0.0), axis=0, keepdims=True)


def decode(level, line):
    rows = level.shape[0]
    wide = jnp.broadcast_to(line, (rows, LANES))
    top = jnp.sum(jnp.where(diagonal(rows), wide, 0.0), axis=1, keepdims=True)
    return level.astype(jnp.int32).astype(jnp.float32) * (top * (1.0 / LEVELS))


def spread_meta(off_ref, on_ref, meta_ref, points):
    def spread(line):
        return jnp.transpose(jnp.broadcast_to(line, (LANES, points)))

    meta_ref[0] = spread(off_ref[0:1, :])
    meta_ref[1] = spread(off_ref[1:2, :])
    meta_ref[2] = spread(on_ref[0:1, :])


def place_windows(pupil_ref, meta_ref, a_ref, a_row, first, points, base_row, rows):
    per = LANES // PB
    chunk = min(64, points)

    def block(index, carry):
        s0 = pl.multiple_of(first + index * chunk, chunk)
        row_off = meta_ref[0, pl.ds(s0, chunk), :]
        col_off = meta_ref[1, pl.ds(s0, chunk), :]
        lit = meta_ref[2, pl.ds(s0, chunk), :].astype(jnp.float32)
        lane = lax.broadcasted_iota(jnp.int32, (chunk, LANES), 1)
        shift = jnp.clip(base_row - row_off, -rows, PB) + rows
        window = pupil_ref[pl.ds(s0, chunk), :].astype(jnp.float32)
        tiles = [None] * (rows // per)
        tiles += [window[:, i * LANES : (i + 1) * LANES] * lit for i in range(PB // per)]
        tiles += [None] * (rows // per)
        zero = jnp.zeros((chunk, LANES), jnp.float32)

        def pick(mask, taken, kept):
            if taken is None and kept is None:
                return None
            return jnp.where(mask, zero if taken is None else taken, zero if kept is None else kept)

        kept_tiles = rows // per + 1
        for bit in reversed(range(((rows + PB) // per).bit_length())):
            step = 1 << bit
            mask = (shift & (step * per)) != 0
            count = kept_tiles + step - 1
            at = lambda i: tiles[i] if i < len(tiles) else None
            tiles = [pick(mask, at(i + step), at(i)) for i in range(count)]
        for step in (2, 1):
            mask = (shift & step) != 0
            turned = [None if t is None else pltpu.roll(t, LANES - PB * step, 1) for t in tiles]
            turned.append(None)
            inside = lane < LANES - PB * step
            moved = [pick(inside, turned[i], turned[i + 1]) for i in range(len(tiles))]
            tiles = [pick(mask, moved[i], tiles[i]) for i in range(len(tiles))]
        tiles = tiles[: rows // per]
        for bit in range(LANES.bit_length() - 1):
            mask = (col_off & (1 << bit)) != 0
            tiles = [jnp.where(mask, pltpu.roll(t, 1 << bit, 1), t) for t in tiles]
        inner = lane - col_off
        covered = (inner >= 0) & (inner < PB)
        for row in range(rows):
            tile, group = tiles[row // per], row % per
            if group:
                tile = pltpu.roll(tile, LANES - PB * group, 1)
            a_ref[pl.ds(a_row + s0, chunk), row * LANES : (row + 1) * LANES] = jnp.where(
                covered, tile, 0.0
            ).astype(jnp.bfloat16)
        return carry

    lax.fori_loop(0, points // chunk, block, 0)


def inverse_factor(packed, size):
    whole = jnp.concatenate([pltpu.roll(packed, size, 1), packed], axis=0)
    full = (8, LANES)
    lane = lax.broadcasted_iota(jnp.int32, full, 1)
    sub = lax.broadcasted_iota(jnp.int32, full, 0)
    unit = jnp.broadcast_to(jnp.broadcast_to(packed[0:8, 0:1], full)[0:1, :], full)
    per_unit = 1.0 / unit
    tiles = []
    for t in range(size // 8):
        eye = jnp.where(lane == sub + 8 * t, 1.0, 0.0)
        tiles.append(jnp.where(lane < size, eye, whole[8 * t : 8 * t + 8] * per_unit))

    def pair(block, k):
        a, b, d = block[k][k], block[k + 1][k], block[k + 1][k + 1]
        per = 1.0 / (a * d - b * b)
        return (d * per, b * per, a * per), b * (1.0 / a)

    def through(inverse, first, second):
        p, q, r = inverse
        return p * first - q * second, r * second - q * first

    wide = 4
    for k in range(0, size, wide):
        home, first = k // 8, k % 8
        columns = [
            [jnp.broadcast_to(tiles[t][:, size + k + j : size + k + j + 1], full) for j in range(wide)]
            for t in range(home, size // 8)
        ]
        lines = [jnp.broadcast_to(tiles[home][first + i : first + i + 1, :], full) for i in range(wide)]
        block = [
            [jnp.broadcast_to(columns[0][j][first + i : first + i + 1, :], full) for j in range(i + 1)]
            for i in range(wide)
        ]
        inverse, ratio = pair(block, 0)
        upper = through(inverse, lines[0], lines[1])
        weights = {}
        for i in (2, 3):
            weights[i] = through(inverse, block[i][0], block[i][1])
            for j in range(2, i + 1):
                block[i][j] = block[i][j] - (weights[i][0] * block[j][0] + weights[i][1] * block[j][1])
            lines[i] = lines[i] - (weights[i][0] * lines[0] + weights[i][1] * lines[1])
        lines[1] = lines[1] - ratio * lines[0]
        inverse, ratio = pair(block, 2)
        lower = through(inverse, lines[2], lines[3])
        lines[3] = lines[3] - ratio * lines[2]
        for t in range(home, size // 8):
            own = columns[t - home]
            third, fourth = (
                own[i] - (own[0] * weights[i][0] + own[1] * weights[i][1]) for i in (2, 3)
            )
            taken = (own[0] * upper[0] + own[1] * upper[1]) + (third * lower[0] + fourth * lower[1])
            updated = tiles[t] - taken
            if t == home:
                updated = jnp.where(sub >= first + wide, updated, tiles[t])
                for i in range(1, wide):
                    updated = jnp.where(sub == first + i, lines[i], updated)
            tiles[t] = updated
    done = []
    for t in range(size // 8):
        pivot = jnp.sum(jnp.where(lane == sub + (8 * t + size), tiles[t], 0.0), axis=1, keepdims=True)
        done.append(tiles[t] * lax.rsqrt(pivot * unit[:, 0:1]))
    return jnp.concatenate(done, axis=0)[:, :size]


def kernel(
    sizes, pupil_hbm, on_hbm, off_hbm, omega_hbm, out_ref,
    pupil_ref, on_ref, off_ref, omega_ref, pupil_far, on_far, off_far, meta, a_ref, cpl_own, cpl_far,
    level, level_top, part_q, part_s, got1_q, got1_s, sum1_q, sum1_s, got2_q, got2_s, sum2_q, sum2_s,
    img_q, img_s, split, gram_out, gram_in, w_far, w_far_in, w_q, w_s, w_in_q, w_in_s,
    setup_send, setup_recv, st_send, st_recv, gram_send, gram_recv, w_send, w_recv, x_send, x_recv,
    c_send, c_recv, f_send, f_recv, load_sem,
):
    n_y, n_z, n_c, n_x = sizes
    my_y, my_z = lax.axis_index("src_0"), lax.axis_index("src_1")
    my_c, my_x = lax.axis_index("src_2"), lax.axis_index("freq")
    other = {"src_2": 1 - my_c}
    rows = G // (n_x * n_c)
    size = omega_hbm.shape[0]
    points = pupil_hbm.shape[0]
    half = rows * G // 2
    quarter = half // 2
    axes = ("src_0", "src_1")
    count = (n_y, n_z)
    mine = (my_y, my_z)
    kept = size // n_y

    def offsets_far_first(n):
        return sorted(range(1, n), key=lambda d: (-min(d, n - d), d))

    group = sorted(
        ((dx, dc) for dx in range(n_x) for dc in range(n_c) if dx or dc),
        key=lambda step: -min(step[0], n_x - step[0]),
    )

    def group_peer(dx, dc):
        peer_x = lax.rem(my_x + dx, n_x)
        peer_c = lax.rem(my_c + dc, n_c)
        return peer_x, peer_c

    barrier = pltpu.get_barrier_semaphore()
    for a in range(2):
        for d in range(1, count[a]):
            pl.semaphore_signal(
                barrier, inc=1, device_id={axes[a]: lax.rem(mine[a] + d, count[a])},
                device_id_type=MESH_ID,
            )
    for dx, dc in group:
        peer_x, peer_c = group_peer(dx, dc)
        pl.semaphore_signal(
            barrier, inc=1, device_id={"freq": peer_x, "src_2": peer_c}, device_id_type=MESH_ID
        )
    local = [
        pltpu.make_async_copy(src, dst, load_sem.at[i])
        for i, (src, dst) in enumerate(
            ((off_hbm, off_ref), (on_hbm, on_ref), (omega_hbm, omega_ref), (pupil_hbm, pupil_ref))
        )
    ]
    for copy in local:
        copy.start()
    pl.semaphore_wait(barrier, n_y - 1 + n_z - 1 + len(group))

    def remote(src, dst, send, recv, device):
        return pltpu.make_async_remote_copy(
            src_ref=src, dst_ref=dst, send_sem=send, recv_sem=recv,
            device_id=device, device_id_type=MESH_ID,
        )

    parts = [pl.ds(0, points // 2), pl.ds(points // 2, points // 2)]
    setup = [
        remote(src, dst, setup_send.at[i], setup_recv.at[i], other)
        for i, (src, dst) in enumerate(
            ((off_hbm, off_far), (on_hbm, on_far), (omega_hbm, cpl_far.at[0]),
             *((pupil_hbm.at[part], pupil_far.at[part]) for part in parts))
        )
    ]
    for copy in setup:
        copy.start()
    for copy in local:
        copy.wait()
    base_row = my_x * (rows * n_c) + my_c * rows
    spread_meta(off_ref, on_ref, meta, points)
    place_windows(pupil_ref, meta, a_ref, 0, 0, points, base_row, rows)
    for copy in setup[:-1]:
        copy.wait_recv()
    spread_meta(off_far, on_far, meta, points)
    place_windows(pupil_far, meta, a_ref, points, 0, points // 2, base_row, rows)
    setup[-1].wait_recv()
    place_windows(pupil_far, meta, a_ref, points, points // 2, points // 2, base_row, rows)
    pending = list(setup)

    outgoing = ((part_q, part_s), (sum1_q, sum1_s), (sum2_q, sum2_s))
    incoming = ((got1_q, got1_s), (got2_q, got2_s), (img_q, img_s))

    def ring(which, h):
        along = h if which != 1 else 1 - h
        return count[along], mine[along], axes[along]

    def stage(it, which, h):
        n, me, name = ring(which, h)
        for d in offsets_far_first(n):
            peer = lax.rem(me + d, n)
            slot = (which * 2 + h) * n
            for i in range(2):
                src = outgoing[which][i].at[it, h]
                copy = remote(
                    src.at[peer] if which == 0 else src, incoming[which][i].at[it, h, me],
                    st_send.at[it, i, slot + peer], st_recv.at[it, i, slot + me], {name: peer},
                )
                copy.start()
                pending.append(copy)
        for i in range(2):
            src = outgoing[which][i].at[it, h]
            incoming[which][i][it, h, me] = src[me] if which == 0 else src[...]

    def arrive(it, which, h, peer):
        n, me, name = ring(which, h)
        slot = (which * 2 + h) * n
        for i in range(2):
            into = incoming[which][i].at[it, h, peer]
            remote(
                into, into, st_send.at[it, i, slot + peer], st_recv.at[it, i, slot + peer],
                {name: peer},
            ).wait_recv()

    def total_of(it, which, h):
        n, me, name = ring(which, h)
        levels, lines = incoming[which]
        if which == 0:
            total = decode(levels[it, h, me], lines[it, h, me])
            for d in offsets_far_first(n):
                peer = lax.rem(me + d, n)
                arrive(it, which, h, peer)
                total = total + decode(levels[it, h, peer], lines[it, h, peer])
        else:
            for d in offsets_far_first(n):
                arrive(it, which, h, lax.rem(me + d, n))
            total = decode(levels[it, h, 0], lines[it, h, 0])
            for p in range(1, n):
                total = total + decode(levels[it, h, p], lines[it, h, p])
        value, top = encode(total)
        levels, lines = outgoing[which + 1]
        levels[it, h] = value.astype(jnp.int16)
        lines[it, h] = column_to_line(top)

    def split_images(slot, h, to, waits):
        together = max(1, 16 // kept)
        n, me, name = ring(2, h)
        teams = n // together
        for step in range(teams):
            if waits:
                g = lax.rem(me // together + step, teams) * together
                for i in range(together):
                    if step:
                        arrive(slot, 2, h, g + i)
                    else:
                        for d in range(1, together):
                            arrive(slot, 2, h, g + lax.rem(me + d, together)) if i == 0 else None
            else:
                g = step * together
            values = [decode(img_q[slot, h, g + i], img_s[slot, h, g + i]) for i in range(together)]
            base = pl.multiple_of(g * kept, together * kept) if waits else g * kept
            for b in range(2):
                part = [v[b * kept : (b + 1) * kept] for v in values]
                high, low = split2(jnp.concatenate(part, axis=0) if together > 1 else part[0])
                cols = slice(h * half + b * quarter, h * half + (b + 1) * quarter)
                split[to, pl.ds(base, together * kept), cols] = high
                split[to, pl.ds(size + base, together * kept), cols] = low

    for it in range(ITERS):
        last = it == ITERS - 1
        left_own = omega_ref[...] if it == 0 else cpl_own[it]
        if it > 0:
            remote(cpl_own.at[it], cpl_far.at[it], c_send.at[it], c_recv.at[it], other).wait_recv()
        left_far = cpl_far[it]
        for h in range(2):
            for b in range(2):
                cols = slice(h * half + b * quarter, h * half + (b + 1) * quarter)
                total = dot_nn(left_own, a_ref[0:points, cols]) + dot_nn(
                    left_far, a_ref[points : 2 * points, cols]
                )
                value, top = encode(total)
                level[:, b * kept : (b + 1) * kept, :] = value.reshape(n_y, kept, quarter)
                level_top[:, b * kept : (b + 1) * kept, :] = jnp.broadcast_to(
                    top, (size, LANES)
                ).reshape(n_y, kept, LANES)
            for g in range(n_y):
                part_q[it, h, g] = level[g].astype(jnp.int16)
                part_s[it, h, g] = column_to_line(level_top[g][:, 0:1])
            stage(it, 0, h)
        for h in range(2):
            total_of(it, 0, h)
            stage(it, 1, h)
        for h in range(2):
            total_of(it, 1, h)
            stage(it, 2, h)
        for h in range(2):
            split_images(it, h, 0, True)
        if last:
            final = [
                remote(img_q.at[it], img_q.at[it + 1], f_send.at[0], f_recv.at[0], other),
                remote(img_s.at[it], img_s.at[it + 1], f_send.at[1], f_recv.at[1], other),
            ]
            for copy in final:
                copy.start()
        both = split[0]
        square = dot_nt(both, both)
        square = square[:size] + square[size:]
        square = square + pltpu.roll(square, size, 1)
        lane = lax.broadcasted_iota(jnp.int32, (size // 2, LANES), 1)
        packed = jnp.where(lane < size, square[: size // 2], square[size // 2 :])
        gram_out[it] = packed
        my_slot = my_x * n_c + my_c
        gram_in[it, my_slot] = packed
        for i, (dx, dc) in enumerate(group):
            peer_x, peer_c = group_peer(dx, dc)
            copy = remote(
                gram_out.at[it], gram_in.at[it, my_slot], gram_send.at[it, i],
                gram_recv.at[it, my_slot], {"freq": peer_x, "src_2": peer_c},
            )
            copy.start()
            pending.append(copy)
        if not last:
            far = dot_nt(both, a_ref[points : 2 * points, :])
            w_far[it] = far[:size] + far[size:]
            swap = remote(w_far.at[it], w_far_in.at[it], w_send.at[it], w_recv.at[it], other)
            swap.start()
            pending.append(swap)
            own = dot_nt(both, a_ref[0:points, :])
            own = own[:size] + own[size:]
            swap.wait_recv()
            own = own + w_far_in[it]
            value, top = encode(own)
            w_q[it] = value.astype(jnp.int16)
            w_s[it] = column_to_line(top)
            for d in offsets_far_first(n_x):
                peer = lax.rem(my_x + d, n_x)
                for i, (src, dst) in enumerate(((w_q, w_in_q), (w_s, w_in_s))):
                    copy = remote(
                        src.at[it], dst.at[it, my_x], x_send.at[it, i, d], x_recv.at[it, i, my_x],
                        {"freq": peer},
                    )
                    copy.start()
                    pending.append(copy)
            w_in_q[it, my_x] = w_q[it]
            w_in_s[it, my_x] = w_s[it]
        else:
            for copy in final:
                copy.wait_recv()
            pending.extend(final)
            for h in range(2):
                split_images(it + 1, h, 1, False)
        for dx, dc in group:
            peer_x, peer_c = group_peer(dx, dc)
            slot = peer_x * n_c + peer_c
            remote(
                gram_out.at[it], gram_in.at[it, slot], gram_send.at[it, 0], gram_recv.at[it, slot],
                {"freq": peer_x, "src_2": peer_c},
            ).wait_recv()
        total = gram_in[it, 0]
        for p in range(1, n_x * n_c):
            total = total + gram_in[it, p]
        inv_high, inv_low = split2(inverse_factor(total * (1.0 / (G * G)), size))
        if not last:
            for d in offsets_far_first(n_x):
                peer = lax.rem(my_x + d, n_x)
                for i, dst in enumerate((w_in_q, w_in_s)):
                    remote(
                        dst.at[it, peer], dst.at[it, peer], x_send.at[it, i, d],
                        x_recv.at[it, i, peer], {"freq": peer},
                    ).wait_recv()
            total = decode(w_in_q[it, 0], w_in_s[it, 0])
            for p in range(1, n_x):
                total = total + decode(w_in_q[it, p], w_in_s[it, p])
            high, low = split2(total)
            cpl_own[it + 1] = apply_factor(inv_high, inv_low, high, low).astype(jnp.bfloat16)
            copy = remote(
                cpl_own.at[it + 1], cpl_far.at[it + 1], c_send.at[it + 1], c_recv.at[it + 1], other
            )
            copy.start()
            pending.append(copy)
        else:
            width = min(256, half)
            for c in range(2):
                slot = jnp.where(my_c == c, 0, 1)
                for j in range(2 * half // width):
                    cols = slice(j * width, (j + 1) * width)
                    start = c * 2 * half + j * width
                    out_ref[:, start : start + width] = apply_factor(
                        inv_high, inv_low, split[slot, 0:size, cols], split[slot, size : 2 * size, cols]
                    )
    for copy in pending:
        copy.wait_send()


def shards(pupil_block, source_on, offsets, omega):
    points = pupil_block.shape[0]
    size = omega.shape[1]
    n_y, n_z, n_c = (lax.axis_size(name) for name in SRC)
    n_x = lax.axis_size("freq")
    rows = G // (n_x * n_c)
    freqs = rows * G
    assert n_y == n_z and n_c == 2
    tall, quarter = 2 * (size // n_y), freqs // 4
    f32, bf16, i32, i16 = jnp.float32, jnp.bfloat16, jnp.int32, jnp.int16
    vmem = pltpu.VMEM
    dma = pltpu.SemaphoreType.DMA

    def blocks(*lead):
        return [vmem((*lead, tall, quarter), i16), vmem((*lead, 1, LANES), f32)]

    scratch = [
        vmem((points, PB * PB), bf16), vmem((1, points), i32), vmem((2, points), i32),
        vmem((size, points), bf16),
        vmem((points, PB * PB), bf16), vmem((1, points), i32), vmem((2, points), i32),
        vmem((3, points, LANES), i32),
        vmem((2 * points, freqs), bf16),
        vmem((ITERS, size, points), bf16), vmem((ITERS, size, points), bf16),
        vmem((n_y, tall, quarter), i32), vmem((n_y, tall, LANES), f32),
        *blocks(ITERS, 2, n_y), *blocks(ITERS, 2, n_y), *blocks(ITERS, 2), *blocks(ITERS, 2, n_z),
        *blocks(ITERS, 2), *blocks(ITERS + 1, 2, n_y),
        vmem((2, 2 * size, freqs), bf16),
        vmem((ITERS, size // 2, LANES), f32), vmem((ITERS, n_x * n_c, size // 2, LANES), f32),
        vmem((ITERS, size, points), f32), vmem((ITERS, size, points), f32),
        vmem((ITERS, size, points), i16), vmem((ITERS, 1, LANES), f32),
        vmem((ITERS, n_x, size, points), i16), vmem((ITERS, n_x, 1, LANES), f32),
        dma((5,)), dma((5,)), dma((ITERS, 2, 6 * n_y)), dma((ITERS, 2, 6 * n_y)),
        dma((ITERS, n_x * n_c)), dma((ITERS, n_x * n_c)), dma((ITERS,)), dma((ITERS,)),
        dma((ITERS, 2, n_x)), dma((ITERS, 2, n_x)), dma((ITERS,)), dma((ITERS,)), dma((2,)), dma((2,)),
        dma((4,)),
    ]
    out = pl.pallas_call(
        functools.partial(kernel, (n_y, n_z, n_c, n_x)),
        out_shape=jax.ShapeDtypeStruct((size, freqs * n_c), f32),
        in_specs=[pl.BlockSpec(memory_space=pltpu.HBM)] * 4,
        out_specs=pl.BlockSpec(memory_space=pltpu.VMEM),
        scratch_shapes=scratch,
        compiler_params=pltpu.CompilerParams(
            collective_id=0, has_side_effects=True, vmem_limit_bytes=14 * 1024 * 1024
        ),
    )(
        *(
            pltpu.with_memory_space_constraint(value, pltpu.HBM)
            for value in (pupil_block, source_on.reshape(1, points), offsets, omega.T)
        )
    )
    return out.T


def solution(mesh):
    split = Mesh(
        mesh.devices.reshape(8, 8, 2, mesh.shape["freq"]), ("src_0", "src_1", "src_2", "freq")
    )
    return jax.shard_map(
        shards,
        mesh=split,
        in_specs=(P(SRC, None), P(SRC), P(None, SRC), P(SRC, None)),
        out_specs=P("freq", None),
        check_vma=False,
    )
```

```python
import functools

import jax
import jax.numpy as jnp
from jax import lax
from jax.experimental import pallas as pl
from jax.experimental.pallas import tpu as pltpu
from jax.sharding import Mesh
from jax.sharding import PartitionSpec as P

G = 128
PB = 32
ITERS = 3
LANES = 128
LEVELS = 32700.0
TINY = 1e-30
SRC = ("src_0", "src_1", "src_2")
MESH_ID = pl.DeviceIdType.MESH


def split2(value):
    high = value.astype(jnp.bfloat16)
    low = (value - high.astype(jnp.float32)).astype(jnp.bfloat16)
    return high, low


def dot_nn(left, right):
    return lax.dot_general(
        left, right, (((1,), (0,)), ((), ())), preferred_element_type=jnp.float32
    )


def dot_nt(left, right):
    return lax.dot_general(
        left, right, (((1,), (1,)), ((), ())), preferred_element_type=jnp.float32
    )


def apply_factor(inv_high, inv_low, high, low):
    return dot_nn(inv_high, high) + (dot_nn(inv_high, low) + dot_nn(inv_low, high))


def encode(value):
    top = jnp.maximum(jnp.max(jnp.abs(value), axis=1, keepdims=True), TINY)
    level = lax.round(value * (LEVELS / top), lax.RoundingMethod.TO_NEAREST_EVEN)
    return level.astype(jnp.int32), top


def diagonal(rows):
    shape = (rows, LANES)
    return lax.broadcasted_iota(jnp.int32, shape, 1) == lax.broadcasted_iota(jnp.int32, shape, 0)


def column_to_line(top):
    rows = top.shape[0]
    wide = jnp.broadcast_to(top, (rows, LANES))
    return jnp.sum(jnp.where(diagonal(rows), wide, 0.0), axis=0, keepdims=True)


def decode(level, line):
    rows = level.shape[0]
    wide = jnp.broadcast_to(line, (rows, LANES))
    top = jnp.sum(jnp.where(diagonal(rows), wide, 0.0), axis=1, keepdims=True)
    return level.astype(jnp.int32).astype(jnp.float32) * (top * (1.0 / LEVELS))


def spread_meta(off_ref, on_ref, meta_ref, points):
    def spread(line):
        return jnp.transpose(jnp.broadcast_to(line, (LANES, points)))

    meta_ref[0] = spread(off_ref[0:1, :])
    meta_ref[1] = spread(off_ref[1:2, :])
    meta_ref[2] = spread(on_ref[0:1, :])


def place_windows(pupil_ref, meta_ref, a_ref, a_row, first, points, base_row, rows):
    per = LANES // PB
    chunk = min(64, points)

    def block(index, carry):
        s0 = pl.multiple_of(first + index * chunk, chunk)
        row_off = meta_ref[0, pl.ds(s0, chunk), :]
        col_off = meta_ref[1, pl.ds(s0, chunk), :]
        lit = meta_ref[2, pl.ds(s0, chunk), :].astype(jnp.float32)
        lane = lax.broadcasted_iota(jnp.int32, (chunk, LANES), 1)
        shift = jnp.clip(base_row - row_off, -rows, PB) + rows
        window = pupil_ref[pl.ds(s0, chunk), :].astype(jnp.float32)
        tiles = [None] * (rows // per)
        tiles += [window[:, i * LANES : (i + 1) * LANES] * lit for i in range(PB // per)]
        tiles += [None] * (rows // per)
        zero = jnp.zeros((chunk, LANES), jnp.float32)

        def pick(mask, taken, kept):
            if taken is None and kept is None:
                return None
            return jnp.where(mask, zero if taken is None else taken, zero if kept is None else kept)

        kept_tiles = rows // per + 1
        for bit in reversed(range(((rows + PB) // per).bit_length())):
            step = 1 << bit
            mask = (shift & (step * per)) != 0
            count = kept_tiles + step - 1
            at = lambda i: tiles[i] if i < len(tiles) else None
            tiles = [pick(mask, at(i + step), at(i)) for i in range(count)]
        for step in (2, 1):
            mask = (shift & step) != 0
            turned = [None if t is None else pltpu.roll(t, LANES - PB * step, 1) for t in tiles]
            turned.append(None)
            inside = lane < LANES - PB * step
            moved = [pick(inside, turned[i], turned[i + 1]) for i in range(len(tiles))]
            tiles = [pick(mask, moved[i], tiles[i]) for i in range(len(tiles))]
        tiles = tiles[: rows // per]
        for bit in range(LANES.bit_length() - 1):
            mask = (col_off & (1 << bit)) != 0
            tiles = [jnp.where(mask, pltpu.roll(t, 1 << bit, 1), t) for t in tiles]
        inner = lane - col_off
        covered = (inner >= 0) & (inner < PB)
        for row in range(rows):
            tile, group = tiles[row // per], row % per
            if group:
                tile = pltpu.roll(tile, LANES - PB * group, 1)
            a_ref[pl.ds(a_row + s0, chunk), row * LANES : (row + 1) * LANES] = jnp.where(
                covered, tile, 0.0
            ).astype(jnp.bfloat16)
        return carry

    lax.fori_loop(0, points // chunk, block, 0)


def inverse_factor(packed, size):
    whole = jnp.concatenate([pltpu.roll(packed, size, 1), packed], axis=0)
    full = (8, LANES)
    lane = lax.broadcasted_iota(jnp.int32, full, 1)
    sub = lax.broadcasted_iota(jnp.int32, full, 0)
    unit = jnp.broadcast_to(jnp.broadcast_to(packed[0:8, 0:1], full)[0:1, :], full)
    per_unit = 1.0 / unit
    tiles = []
    for t in range(size // 8):
        eye = jnp.where(lane == sub + 8 * t, 1.0, 0.0)
        tiles.append(jnp.where(lane < size, eye, whole[8 * t : 8 * t + 8] * per_unit))

    def pair(block, k):
        a, b, d = block[k][k], block[k + 1][k], block[k + 1][k + 1]
        per = 1.0 / (a * d - b * b)
        return (d * per, b * per, a * per), b * (1.0 / a)

    def through(inverse, first, second):
        p, q, r = inverse
        return p * first - q * second, r * second - q * first

    wide = 4
    for k in range(0, size, wide):
        home, first = k // 8, k % 8
        columns = [
            [jnp.broadcast_to(tiles[t][:, size + k + j : size + k + j + 1], full) for j in range(wide)]
            for t in range(home, size // 8)
        ]
        lines = [jnp.broadcast_to(tiles[home][first + i : first + i + 1, :], full) for i in range(wide)]
        block = [
            [jnp.broadcast_to(columns[0][j][first + i : first + i + 1, :], full) for j in range(i + 1)]
            for i in range(wide)
        ]
        inverse, ratio = pair(block, 0)
        upper = through(inverse, lines[0], lines[1])
        weights = {}
        for i in (2, 3):
            weights[i] = through(inverse, block[i][0], block[i][1])
            for j in range(2, i + 1):
                block[i][j] = block[i][j] - (weights[i][0] * block[j][0] + weights[i][1] * block[j][1])
            lines[i] = lines[i] - (weights[i][0] * lines[0] + weights[i][1] * lines[1])
        lines[1] = lines[1] - ratio * lines[0]
        inverse, ratio = pair(block, 2)
        lower = through(inverse, lines[2], lines[3])
        lines[3] = lines[3] - ratio * lines[2]
        for t in range(home, size // 8):
            own = columns[t - home]
            third, fourth = (
                own[i] - (own[0] * weights[i][0] + own[1] * weights[i][1]) for i in (2, 3)
            )
            taken = (own[0] * upper[0] + own[1] * upper[1]) + (third * lower[0] + fourth * lower[1])
            updated = tiles[t] - taken
            if t == home:
                updated = jnp.where(sub >= first + wide, updated, tiles[t])
                for i in range(1, wide):
                    updated = jnp.where(sub == first + i, lines[i], updated)
            tiles[t] = updated
    done = []
    for t in range(size // 8):
        pivot = jnp.sum(jnp.where(lane == sub + (8 * t + size), tiles[t], 0.0), axis=1, keepdims=True)
        done.append(tiles[t] * lax.rsqrt(pivot * unit[:, 0:1]))
    return jnp.concatenate(done, axis=0)[:, :size]


def kernel(
    sizes, pupil_hbm, on_hbm, off_hbm, omega_hbm, out_ref,
    pupil_ref, on_ref, off_ref, omega_ref, pupil_far, on_far, off_far, meta, a_ref, cpl_own, cpl_far,
    level, level_top, part_q, part_s, got1_q, got1_s, sum1_q, sum1_s, got2_q, got2_s, sum2_q, sum2_s,
    img_q, img_s, split, gram_out, gram_in, w_far, w_far_in, w_q, w_s, w_in_q, w_in_s,
    setup_send, setup_recv, st_send, st_recv, gram_send, gram_recv, w_send, w_recv, x_send, x_recv,
    c_send, c_recv, f_send, f_recv, load_sem,
):
    n_y, n_z, n_c, n_x = sizes
    my_y, my_z = lax.axis_index("src_0"), lax.axis_index("src_1")
    my_c, my_x = lax.axis_index("src_2"), lax.axis_index("freq")
    other = {"src_2": 1 - my_c}
    rows = G // (n_x * n_c)
    size = omega_hbm.shape[0]
    points = pupil_hbm.shape[0]
    half = rows * G // 2
    quarter = half // 2
    axes = ("src_0", "src_1")
    count = (n_y, n_z)
    mine = (my_y, my_z)
    kept = size // n_y

    def offsets_far_first(n):
        return sorted(range(1, n), key=lambda d: (-min(d, n - d), d))

    group = sorted(
        ((dx, dc) for dx in range(n_x) for dc in range(n_c) if dx or dc),
        key=lambda step: -min(step[0], n_x - step[0]),
    )

    def group_peer(dx, dc):
        peer_x = lax.rem(my_x + dx, n_x)
        peer_c = lax.rem(my_c + dc, n_c)
        return peer_x, peer_c

    barrier = pltpu.get_barrier_semaphore()
    for a in range(2):
        for d in range(1, count[a]):
            pl.semaphore_signal(
                barrier, inc=1, device_id={axes[a]: lax.rem(mine[a] + d, count[a])},
                device_id_type=MESH_ID,
            )
    for dx, dc in group:
        peer_x, peer_c = group_peer(dx, dc)
        pl.semaphore_signal(
            barrier, inc=1, device_id={"freq": peer_x, "src_2": peer_c}, device_id_type=MESH_ID
        )
    local = [
        pltpu.make_async_copy(src, dst, load_sem.at[i])
        for i, (src, dst) in enumerate(
            ((off_hbm, off_ref), (on_hbm, on_ref), (omega_hbm, omega_ref), (pupil_hbm, pupil_ref))
        )
    ]
    for copy in local:
        copy.start()
    pl.semaphore_wait(barrier, n_y - 1 + n_z - 1 + len(group))

    def remote(src, dst, send, recv, device):
        return pltpu.make_async_remote_copy(
            src_ref=src, dst_ref=dst, send_sem=send, recv_sem=recv,
            device_id=device, device_id_type=MESH_ID,
        )

    parts = [pl.ds(0, points // 2), pl.ds(points // 2, points // 2)]
    setup = [
        remote(src, dst, setup_send.at[i], setup_recv.at[i], other)
        for i, (src, dst) in enumerate(
            ((off_hbm, off_far), (on_hbm, on_far), (omega_hbm, cpl_far.at[0]),
             *((pupil_hbm.at[part], pupil_far.at[part]) for part in parts))
        )
    ]
    for copy in setup:
        copy.start()
    for copy in local:
        copy.wait()
    base_row = my_x * (rows * n_c) + my_c * rows
    spread_meta(off_ref, on_ref, meta, points)
    place_windows(pupil_ref, meta, a_ref, 0, 0, points, base_row, rows)
    for copy in setup[:-1]:
        copy.wait_recv()
    spread_meta(off_far, on_far, meta, points)
    place_windows(pupil_far, meta, a_ref, points, 0, points // 2, base_row, rows)
    setup[-1].wait_recv()
    place_windows(pupil_far, meta, a_ref, points, points // 2, points // 2, base_row, rows)
    pending = list(setup)

    outgoing = ((part_q, part_s), (sum1_q, sum1_s), (sum2_q, sum2_s))
    incoming = ((got1_q, got1_s), (got2_q, got2_s), (img_q, img_s))

    def ring(which, h):
        along = h if which != 1 else 1 - h
        return count[along], mine[along], axes[along]

    def stage(it, which, h):
        n, me, name = ring(which, h)
        for d in offsets_far_first(n):
            peer = lax.rem(me + d, n)
            slot = (which * 2 + h) * n
            for i in range(2):
                src = outgoing[which][i].at[it, h]
                copy = remote(
                    src.at[peer] if which == 0 else src, incoming[which][i].at[it, h, me],
                    st_send.at[it, i, slot + peer], st_recv.at[it, i, slot + me], {name: peer},
                )
                copy.start()
                pending.append(copy)
        for i in range(2):
            src = outgoing[which][i].at[it, h]
            incoming[which][i][it, h, me] = src[me] if which == 0 else src[...]

    def arrive(it, which, h):
        n, me, name = ring(which, h)
        for d in offsets_far_first(n):
            peer = lax.rem(me + d, n)
            slot = (which * 2 + h) * n
            for i in range(2):
                into = incoming[which][i].at[it, h, peer]
                remote(
                    into, into, st_send.at[it, i, slot + peer], st_recv.at[it, i, slot + peer],
                    {name: peer},
                ).wait_recv()

    def total_of(it, which, h):
        n = ring(which, h)[0]
        levels, lines = incoming[which]
        total = decode(levels[it, h, 0], lines[it, h, 0])
        for p in range(1, n):
            total = total + decode(levels[it, h, p], lines[it, h, p])
        value, top = encode(total)
        levels, lines = outgoing[which + 1]
        levels[it, h] = value.astype(jnp.int16)
        lines[it, h] = column_to_line(top)

    def split_images(slot, h, to):
        together = max(1, 16 // kept)
        for g in range(0, n_y, together):
            values = [decode(img_q[slot, h, g + i], img_s[slot, h, g + i]) for i in range(together)]
            for b in range(2):
                part = [v[b * kept : (b + 1) * kept] for v in values]
                high, low = split2(jnp.concatenate(part, axis=0) if together > 1 else part[0])
                cols = slice(h * half + b * quarter, h * half + (b + 1) * quarter)
                split[to, g * kept : (g + together) * kept, cols] = high
                split[to, size + g * kept : size + (g + together) * kept, cols] = low

    for it in range(ITERS):
        last = it == ITERS - 1
        left_own = omega_ref[...] if it == 0 else cpl_own[it]
        if it > 0:
            remote(cpl_own.at[it], cpl_far.at[it], c_send.at[it], c_recv.at[it], other).wait_recv()
        left_far = cpl_far[it]
        for h in range(2):
            for b in range(2):
                cols = slice(h * half + b * quarter, h * half + (b + 1) * quarter)
                total = dot_nn(left_own, a_ref[0:points, cols]) + dot_nn(
                    left_far, a_ref[points : 2 * points, cols]
                )
                value, top = encode(total)
                level[:, b * kept : (b + 1) * kept, :] = value.reshape(n_y, kept, quarter)
                level_top[:, b * kept : (b + 1) * kept, :] = jnp.broadcast_to(
                    top, (size, LANES)
                ).reshape(n_y, kept, LANES)
            for g in range(n_y):
                part_q[it, h, g] = level[g].astype(jnp.int16)
                part_s[it, h, g] = column_to_line(level_top[g][:, 0:1])
            stage(it, 0, h)
        for h in range(2):
            arrive(it, 0, h)
            total_of(it, 0, h)
            stage(it, 1, h)
        for h in range(2):
            arrive(it, 1, h)
            total_of(it, 1, h)
            stage(it, 2, h)
        for h in range(2):
            arrive(it, 2, h)
            split_images(it, h, 0)
        if last:
            final = [
                remote(img_q.at[it], img_q.at[it + 1], f_send.at[0], f_recv.at[0], other),
                remote(img_s.at[it], img_s.at[it + 1], f_send.at[1], f_recv.at[1], other),
            ]
            for copy in final:
                copy.start()
        both = split[0]
        square = dot_nt(both, both)
        square = square[:size] + square[size:]
        square = square + pltpu.roll(square, size, 1)
        lane = lax.broadcasted_iota(jnp.int32, (size // 2, LANES), 1)
        packed = jnp.where(lane < size, square[: size // 2], square[size // 2 :])
        gram_out[it] = packed
        my_slot = my_x * n_c + my_c
        gram_in[it, my_slot] = packed
        for i, (dx, dc) in enumerate(group):
            peer_x, peer_c = group_peer(dx, dc)
            copy = remote(
                gram_out.at[it], gram_in.at[it, my_slot], gram_send.at[it, i],
                gram_recv.at[it, my_slot], {"freq": peer_x, "src_2": peer_c},
            )
            copy.start()
            pending.append(copy)
        if not last:
            far = dot_nt(both, a_ref[points : 2 * points, :])
            w_far[it] = far[:size] + far[size:]
            swap = remote(w_far.at[it], w_far_in.at[it], w_send.at[it], w_recv.at[it], other)
            swap.start()
            pending.append(swap)
            own = dot_nt(both, a_ref[0:points, :])
            own = own[:size] + own[size:]
            swap.wait_recv()
            own = own + w_far_in[it]
            value, top = encode(own)
            w_q[it] = value.astype(jnp.int16)
            w_s[it] = column_to_line(top)
            for d in offsets_far_first(n_x):
                peer = lax.rem(my_x + d, n_x)
                for i, (src, dst) in enumerate(((w_q, w_in_q), (w_s, w_in_s))):
                    copy = remote(
                        src.at[it], dst.at[it, my_x], x_send.at[it, i, d], x_recv.at[it, i, my_x],
                        {"freq": peer},
                    )
                    copy.start()
                    pending.append(copy)
            w_in_q[it, my_x] = w_q[it]
            w_in_s[it, my_x] = w_s[it]
        else:
            for copy in final:
                copy.wait_recv()
            pending.extend(final)
            for h in range(2):
                split_images(it + 1, h, 1)
        for dx, dc in group:
            peer_x, peer_c = group_peer(dx, dc)
            slot = peer_x * n_c + peer_c
            remote(
                gram_out.at[it], gram_in.at[it, slot], gram_send.at[it, 0], gram_recv.at[it, slot],
                {"freq": peer_x, "src_2": peer_c},
            ).wait_recv()
        total = gram_in[it, 0]
        for p in range(1, n_x * n_c):
            total = total + gram_in[it, p]
        inv_high, inv_low = split2(inverse_factor(total * (1.0 / (G * G)), size))
        if not last:
            for d in offsets_far_first(n_x):
                peer = lax.rem(my_x + d, n_x)
                for i, dst in enumerate((w_in_q, w_in_s)):
                    remote(
                        dst.at[it, peer], dst.at[it, peer], x_send.at[it, i, d],
                        x_recv.at[it, i, peer], {"freq": peer},
                    ).wait_recv()
            total = decode(w_in_q[it, 0], w_in_s[it, 0])
            for p in range(1, n_x):
                total = total + decode(w_in_q[it, p], w_in_s[it, p])
            high, low = split2(total)
            cpl_own[it + 1] = apply_factor(inv_high, inv_low, high, low).astype(jnp.bfloat16)
            copy = remote(
                cpl_own.at[it + 1], cpl_far.at[it + 1], c_send.at[it + 1], c_recv.at[it + 1], other
            )
            copy.start()
            pending.append(copy)
        else:
            width = min(256, half)
            for c in range(2):
                slot = jnp.where(my_c == c, 0, 1)
                for j in range(2 * half // width):
                    cols = slice(j * width, (j + 1) * width)
                    start = c * 2 * half + j * width
                    out_ref[:, start : start + width] = apply_factor(
                        inv_high, inv_low, split[slot, 0:size, cols], split[slot, size : 2 * size, cols]
                    )
    for copy in pending:
        copy.wait_send()


def shards(pupil_block, source_on, offsets, omega):
    points = pupil_block.shape[0]
    size = omega.shape[1]
    n_y, n_z, n_c = (lax.axis_size(name) for name in SRC)
    n_x = lax.axis_size("freq")
    rows = G // (n_x * n_c)
    freqs = rows * G
    assert n_y == n_z and n_c == 2
    tall, quarter = 2 * (size // n_y), freqs // 4
    f32, bf16, i32, i16 = jnp.float32, jnp.bfloat16, jnp.int32, jnp.int16
    vmem = pltpu.VMEM
    dma = pltpu.SemaphoreType.DMA

    def blocks(*lead):
        return [vmem((*lead, tall, quarter), i16), vmem((*lead, 1, LANES), f32)]

    scratch = [
        vmem((points, PB * PB), bf16), vmem((1, points), i32), vmem((2, points), i32),
        vmem((size, points), bf16),
        vmem((points, PB * PB), bf16), vmem((1, points), i32), vmem((2, points), i32),
        vmem((3, points, LANES), i32),
        vmem((2 * points, freqs), bf16),
        vmem((ITERS, size, points), bf16), vmem((ITERS, size, points), bf16),
        vmem((n_y, tall, quarter), i32), vmem((n_y, tall, LANES), f32),
        *blocks(ITERS, 2, n_y), *blocks(ITERS, 2, n_y), *blocks(ITERS, 2), *blocks(ITERS, 2, n_z),
        *blocks(ITERS, 2), *blocks(ITERS + 1, 2, n_y),
        vmem((2, 2 * size, freqs), bf16),
        vmem((ITERS, size // 2, LANES), f32), vmem((ITERS, n_x * n_c, size // 2, LANES), f32),
        vmem((ITERS, size, points), f32), vmem((ITERS, size, points), f32),
        vmem((ITERS, size, points), i16), vmem((ITERS, 1, LANES), f32),
        vmem((ITERS, n_x, size, points), i16), vmem((ITERS, n_x, 1, LANES), f32),
        dma((5,)), dma((5,)), dma((ITERS, 2, 6 * n_y)), dma((ITERS, 2, 6 * n_y)),
        dma((ITERS, n_x * n_c)), dma((ITERS, n_x * n_c)), dma((ITERS,)), dma((ITERS,)),
        dma((ITERS, 2, n_x)), dma((ITERS, 2, n_x)), dma((ITERS,)), dma((ITERS,)), dma((2,)), dma((2,)),
        dma((4,)),
    ]
    out = pl.pallas_call(
        functools.partial(kernel, (n_y, n_z, n_c, n_x)),
        out_shape=jax.ShapeDtypeStruct((size, freqs * n_c), f32),
        in_specs=[pl.BlockSpec(memory_space=pltpu.HBM)] * 4,
        out_specs=pl.BlockSpec(memory_space=pltpu.VMEM),
        scratch_shapes=scratch,
        compiler_params=pltpu.CompilerParams(
            collective_id=0, has_side_effects=True, vmem_limit_bytes=14 * 1024 * 1024
        ),
    )(
        *(
            pltpu.with_memory_space_constraint(value, pltpu.HBM)
            for value in (pupil_block, source_on.reshape(1, points), offsets, omega.T)
        )
    )
    return out.T


def solution(mesh):
    split = Mesh(
        mesh.devices.reshape(8, 8, 2, mesh.shape["freq"]), ("src_0", "src_1", "src_2", "freq")
    )
    return jax.shard_map(
        shards,
        mesh=split,
        in_specs=(P(SRC, None), P(SRC), P(None, SRC), P(SRC, None)),
        out_specs=P("freq", None),
        check_vma=False,
    )
```

```python
import functools

import jax
import jax.numpy as jnp
from jax import lax
from jax.experimental import pallas as pl
from jax.experimental.pallas import tpu as pltpu
from jax.sharding import Mesh
from jax.sharding import PartitionSpec as P

G = 128
PB = 32
ITERS = 3
LANES = 128
LEVELS = 32700.0
TINY = 1e-30
SRC = ("src_0", "src_1", "src_2")
MESH_ID = pl.DeviceIdType.MESH


def split2(value):
    high = value.astype(jnp.bfloat16)
    low = (value - high.astype(jnp.float32)).astype(jnp.bfloat16)
    return high, low


def dot_nn(left, right):
    return lax.dot_general(
        left, right, (((1,), (0,)), ((), ())), preferred_element_type=jnp.float32
    )


def dot_nt(left, right):
    return lax.dot_general(
        left, right, (((1,), (1,)), ((), ())), preferred_element_type=jnp.float32
    )


def apply_factor(inv_high, inv_low, high, low):
    return dot_nn(inv_high, high) + (dot_nn(inv_high, low) + dot_nn(inv_low, high))


def apply_stacked(inv_twice, inv_low, both):
    return dot_nn(inv_twice, both) + dot_nn(inv_low, both[: both.shape[0] // 2])


def encode(value):
    top = jnp.maximum(jnp.max(jnp.abs(value), axis=1, keepdims=True), TINY)
    level = lax.round(value * (LEVELS / top), lax.RoundingMethod.TO_NEAREST_EVEN)
    return level.astype(jnp.int32), top


def diagonal(rows):
    shape = (rows, LANES)
    return lax.broadcasted_iota(jnp.int32, shape, 1) == lax.broadcasted_iota(jnp.int32, shape, 0)


def column_to_line(top):
    rows = top.shape[0]
    wide = jnp.broadcast_to(top, (rows, LANES))
    return jnp.sum(jnp.where(diagonal(rows), wide, 0.0), axis=0, keepdims=True)


def decode(level, line):
    rows = level.shape[0]
    wide = jnp.broadcast_to(line, (rows, LANES))
    top = jnp.sum(jnp.where(diagonal(rows), wide, 0.0), axis=1, keepdims=True)
    return level.astype(jnp.int32).astype(jnp.float32) * (top * (1.0 / LEVELS))


def spread_meta(off_ref, on_ref, meta_ref, points):
    def spread(line):
        return jnp.transpose(jnp.broadcast_to(line, (LANES, points)))

    meta_ref[0] = spread(off_ref[0:1, :])
    meta_ref[1] = spread(off_ref[1:2, :])
    meta_ref[2] = spread(on_ref[0:1, :])


def place_windows(pupil_ref, meta_ref, a_ref, a_row, first, points, base_row, rows):
    per = LANES // PB
    chunk = min(64, points)

    def block(index, carry):
        s0 = pl.multiple_of(first + index * chunk, chunk)
        row_off = meta_ref[0, pl.ds(s0, chunk), :]
        col_off = meta_ref[1, pl.ds(s0, chunk), :]
        lit = meta_ref[2, pl.ds(s0, chunk), :].astype(jnp.float32)
        lane = lax.broadcasted_iota(jnp.int32, (chunk, LANES), 1)
        shift = jnp.clip(base_row - row_off, -rows, PB) + rows
        window = pupil_ref[pl.ds(s0, chunk), :].astype(jnp.float32)
        tiles = [None] * (rows // per)
        tiles += [window[:, i * LANES : (i + 1) * LANES] * lit for i in range(PB // per)]
        tiles += [None] * (rows // per)
        zero = jnp.zeros((chunk, LANES), jnp.float32)

        def pick(mask, taken, kept):
            if taken is None and kept is None:
                return None
            return jnp.where(mask, zero if taken is None else taken, zero if kept is None else kept)

        kept_tiles = rows // per + 1
        for bit in reversed(range(((rows + PB) // per).bit_length())):
            step = 1 << bit
            mask = (shift & (step * per)) != 0
            count = kept_tiles + step - 1
            at = lambda i: tiles[i] if i < len(tiles) else None
            tiles = [pick(mask, at(i + step), at(i)) for i in range(count)]
        for step in (2, 1):
            mask = (shift & step) != 0
            turned = [None if t is None else pltpu.roll(t, LANES - PB * step, 1) for t in tiles]
            turned.append(None)
            inside = lane < LANES - PB * step
            moved = [pick(inside, turned[i], turned[i + 1]) for i in range(len(tiles))]
            tiles = [pick(mask, moved[i], tiles[i]) for i in range(len(tiles))]
        tiles = tiles[: rows // per]
        for bit in range(LANES.bit_length() - 1):
            mask = (col_off & (1 << bit)) != 0
            tiles = [jnp.where(mask, pltpu.roll(t, 1 << bit, 1), t) for t in tiles]
        inner = lane - col_off
        covered = (inner >= 0) & (inner < PB)
        for row in range(rows):
            tile, group = tiles[row // per], row % per
            if group:
                tile = pltpu.roll(tile, LANES - PB * group, 1)
            a_ref[pl.ds(a_row + s0, chunk), row * LANES : (row + 1) * LANES] = jnp.where(
                covered, tile, 0.0
            ).astype(jnp.bfloat16)
        return carry

    lax.fori_loop(0, points // chunk, block, 0)


def inverse_factor(packed, size):
    whole = jnp.concatenate([pltpu.roll(packed, size, 1), packed], axis=0)
    full = (8, LANES)
    lane = lax.broadcasted_iota(jnp.int32, full, 1)
    sub = lax.broadcasted_iota(jnp.int32, full, 0)
    unit = jnp.broadcast_to(jnp.broadcast_to(packed[0:8, 0:1], full)[0:1, :], full)
    per_unit = 1.0 / unit
    tiles = []
    for t in range(size // 8):
        eye = jnp.where(lane == sub + 8 * t, 1.0, 0.0)
        tiles.append(jnp.where(lane < size, eye, whole[8 * t : 8 * t + 8] * per_unit))

    def pair(block, k):
        a, b, d = block[k][k], block[k + 1][k], block[k + 1][k + 1]
        per = 1.0 / (a * d - b * b)
        return (d * per, b * per, a * per), b * (1.0 / a)

    def through(inverse, first, second):
        p, q, r = inverse
        return p * first - q * second, r * second - q * first

    wide = 4
    for k in range(0, size, wide):
        home, first = k // 8, k % 8
        columns = [
            [jnp.broadcast_to(tiles[t][:, size + k + j : size + k + j + 1], full) for j in range(wide)]
            for t in range(home, size // 8)
        ]
        lines = [jnp.broadcast_to(tiles[home][first + i : first + i + 1, :], full) for i in range(wide)]
        block = [
            [jnp.broadcast_to(columns[0][j][first + i : first + i + 1, :], full) for j in range(i + 1)]
            for i in range(wide)
        ]
        inverse, ratio = pair(block, 0)
        upper = through(inverse, lines[0], lines[1])
        weights = {}
        for i in (2, 3):
            weights[i] = through(inverse, block[i][0], block[i][1])
            for j in range(2, i + 1):
                block[i][j] = block[i][j] - (weights[i][0] * block[j][0] + weights[i][1] * block[j][1])
            lines[i] = lines[i] - (weights[i][0] * lines[0] + weights[i][1] * lines[1])
        lines[1] = lines[1] - ratio * lines[0]
        inverse, ratio = pair(block, 2)
        lower = through(inverse, lines[2], lines[3])
        lines[3] = lines[3] - ratio * lines[2]
        for t in range(home, size // 8):
            own = columns[t - home]
            third, fourth = (
                own[i] - (own[0] * weights[i][0] + own[1] * weights[i][1]) for i in (2, 3)
            )
            taken = (own[0] * upper[0] + own[1] * upper[1]) + (third * lower[0] + fourth * lower[1])
            updated = tiles[t] - taken
            if t == home:
                updated = jnp.where(sub >= first + wide, updated, tiles[t])
                for i in range(1, wide):
                    updated = jnp.where(sub == first + i, lines[i], updated)
            tiles[t] = updated
    done = []
    for t in range(size // 8):
        pivot = jnp.sum(jnp.where(lane == sub + (8 * t + size), tiles[t], 0.0), axis=1, keepdims=True)
        done.append(tiles[t] * lax.rsqrt(pivot * unit[:, 0:1]))
    return jnp.concatenate(done, axis=0)[:, :size]


def kernel(
    sizes, pupil_hbm, on_hbm, off_hbm, omega_hbm, out_ref,
    pupil_ref, on_ref, off_ref, omega_ref, pupil_far, on_far, off_far, meta, a_ref, cpl_own, cpl_far,
    level, level_top, part_q, part_s, got1_q, got1_s, sum1_q, sum1_s, got2_q, got2_s, sum2_q, sum2_s,
    img_q, img_s, split, gram_out, gram_in, w_far, w_far_in, w_q, w_s, w_in_q, w_in_s,
    setup_send, setup_recv, st_send, st_recv, gram_send, gram_recv, w_send, w_recv, x_send, x_recv,
    c_send, c_recv, f_send, f_recv, load_sem, own_part,
):
    n_y, n_z, n_c, n_x = sizes
    my_y, my_z = lax.axis_index("src_0"), lax.axis_index("src_1")
    my_c, my_x = lax.axis_index("src_2"), lax.axis_index("freq")
    other = {"src_2": 1 - my_c}
    rows = G // (n_x * n_c)
    size = omega_hbm.shape[0]
    points = pupil_hbm.shape[0]
    half = rows * G // 2
    quarter = half // 2
    axes = ("src_0", "src_1")
    count = (n_y, n_z)
    mine = (my_y, my_z)
    kept = size // n_y

    def offsets_far_first(n):
        return sorted(range(1, n), key=lambda d: (-min(d, n - d), d))

    group = sorted(
        ((dx, dc) for dx in range(n_x) for dc in range(n_c) if dx or dc),
        key=lambda step: -min(step[0], n_x - step[0]),
    )

    def group_peer(dx, dc):
        peer_x = lax.rem(my_x + dx, n_x)
        peer_c = lax.rem(my_c + dc, n_c)
        return peer_x, peer_c

    barrier = pltpu.get_barrier_semaphore()
    for a in range(2):
        for d in range(1, count[a]):
            pl.semaphore_signal(
                barrier, inc=1, device_id={axes[a]: lax.rem(mine[a] + d, count[a])},
                device_id_type=MESH_ID,
            )
    for dx, dc in group:
        peer_x, peer_c = group_peer(dx, dc)
        pl.semaphore_signal(
            barrier, inc=1, device_id={"freq": peer_x, "src_2": peer_c}, device_id_type=MESH_ID
        )
    local = [
        pltpu.make_async_copy(src, dst, load_sem.at[i])
        for i, (src, dst) in enumerate(
            ((off_hbm, off_ref), (on_hbm, on_ref), (omega_hbm, omega_ref), (pupil_hbm, pupil_ref))
        )
    ]
    for copy in local:
        copy.start()
    pl.semaphore_wait(barrier, n_y - 1 + n_z - 1 + len(group))

    def remote(src, dst, send, recv, device):
        return pltpu.make_async_remote_copy(
            src_ref=src, dst_ref=dst, send_sem=send, recv_sem=recv,
            device_id=device, device_id_type=MESH_ID,
        )

    parts = [pl.ds(0, points // 2), pl.ds(points // 2, points // 2)]
    setup = [
        remote(src, dst, setup_send.at[i], setup_recv.at[i], other)
        for i, (src, dst) in enumerate(
            ((off_hbm, off_far), (on_hbm, on_far), (omega_hbm, cpl_far.at[0]),
             *((pupil_hbm.at[part], pupil_far.at[part]) for part in parts))
        )
    ]
    for copy in setup:
        copy.start()
    for copy in local:
        copy.wait()
    base_row = my_x * (rows * n_c) + my_c * rows
    spread_meta(off_ref, on_ref, meta, points)
    place_windows(pupil_ref, meta, a_ref, 0, 0, points, base_row, rows)
    for copy in setup[:-1]:
        copy.wait_recv()
    spread_meta(off_far, on_far, meta, points)
    place_windows(pupil_far, meta, a_ref, points, 0, points // 2, base_row, rows)
    setup[-1].wait_recv()
    place_windows(pupil_far, meta, a_ref, points, points // 2, points // 2, base_row, rows)
    pending = list(setup)

    outgoing = ((part_q, part_s), (sum1_q, sum1_s), (sum2_q, sum2_s))
    incoming = ((got1_q, got1_s), (got2_q, got2_s), (img_q, img_s))

    def ring(which, h):
        along = h if which != 1 else 1 - h
        return count[along], mine[along], axes[along]

    def stage(it, which, h, pending):
        n, me, name = ring(which, h)
        for d in offsets_far_first(n):
            peer = lax.rem(me + d, n)
            slot = (which * 2 + h) * n
            for i in range(2):
                src = outgoing[which][i].at[it, h]
                copy = remote(
                    src.at[peer] if which == 0 else src, incoming[which][i].at[it, h, me],
                    st_send.at[it, i, slot + peer], st_recv.at[it, i, slot + me], {name: peer},
                )
                copy.start()
                pending.append(copy)
        for i in range(2):
            src = outgoing[which][i].at[it, h]
            incoming[which][i][it, h, me] = src[me] if which == 0 else src[...]

    def arrive(it, which, h):
        n, me, name = ring(which, h)
        for d in offsets_far_first(n):
            peer = lax.rem(me + d, n)
            slot = (which * 2 + h) * n
            for i in range(2):
                into = incoming[which][i].at[it, h, peer]
                remote(
                    into, into, st_send.at[it, i, slot + peer], st_recv.at[it, i, slot + peer],
                    {name: peer},
                ).wait_recv()

    def total_of(it, which, h):
        n = ring(which, h)[0]
        levels, lines = incoming[which]
        total = decode(levels[it, h, 0], lines[it, h, 0])
        for p in range(1, n):
            total = total + decode(levels[it, h, p], lines[it, h, p])
        value, top = encode(total)
        levels, lines = outgoing[which + 1]
        levels[it, h] = value.astype(jnp.int16)
        lines[it, h] = column_to_line(top)

    def split_images(slot, h, to):
        together = max(1, 16 // kept)
        for g in range(0, n_y, together):
            values = [decode(img_q[slot, h, g + i], img_s[slot, h, g + i]) for i in range(together)]
            for b in range(2):
                part = [v[b * kept : (b + 1) * kept] for v in values]
                high, low = split2(jnp.concatenate(part, axis=0) if together > 1 else part[0])
                cols = slice(h * half + b * quarter, h * half + (b + 1) * quarter)
                split[to, g * kept : (g + together) * kept, cols] = high
                split[to, size + g * kept : size + (g + together) * kept, cols] = low

    for it in range(ITERS):
        last = it == ITERS - 1
        left_own = omega_ref[...] if it == 0 else cpl_own[it]
        blocks = [
            slice(h * half + b * quarter, h * half + (b + 1) * quarter) for h in range(2) for b in range(2)
        ]
        if it > 0:
            for cols in blocks:
                own_part[:, cols] = dot_nn(left_own, a_ref[0:points, cols])
            remote(cpl_own.at[it], cpl_far.at[it], c_send.at[it], c_recv.at[it], other).wait_recv()
        left_far = cpl_far[it]
        for h in range(2):
            for b in range(2):
                cols = blocks[2 * h + b]
                near = own_part[:, cols] if it > 0 else dot_nn(left_own, a_ref[0:points, cols])
                total = near + dot_nn(left_far, a_ref[points : 2 * points, cols])
                value, top = encode(total)
                level[:, b * kept : (b + 1) * kept, :] = value.reshape(n_y, kept, quarter)
                level_top[:, b * kept : (b + 1) * kept, :] = jnp.broadcast_to(
                    top, (size, LANES)
                ).reshape(n_y, kept, LANES)
            for g in range(n_y):
                part_q[it, h, g] = level[g].astype(jnp.int16)
                part_s[it, h, g] = column_to_line(level_top[g][:, 0:1])
            stage(it, 0, h, pending)
        for h in range(2):
            arrive(it, 0, h)
            total_of(it, 0, h)
            stage(it, 1, h, pending)
        for h in range(2):
            arrive(it, 1, h)
            total_of(it, 1, h)
            stage(it, 2, h, pending)
        for h in range(2):
            arrive(it, 2, h)
            split_images(it, h, 0)
        if last:
            final = [
                remote(img_q.at[it], img_q.at[it + 1], f_send.at[0], f_recv.at[0], other),
                remote(img_s.at[it], img_s.at[it + 1], f_send.at[1], f_recv.at[1], other),
            ]
            for copy in final:
                copy.start()
        drained, pending = pending, []
        both = split[0]
        square = dot_nt(both, both)
        square = square[:size] + square[size:]
        square = square + pltpu.roll(square, size, 1)
        lane = lax.broadcasted_iota(jnp.int32, (size // 2, LANES), 1)
        packed = jnp.where(lane < size, square[: size // 2], square[size // 2 :])
        gram_out[it] = packed
        my_slot = my_x * n_c + my_c
        gram_in[it, my_slot] = packed
        for i, (dx, dc) in enumerate(group):
            peer_x, peer_c = group_peer(dx, dc)
            copy = remote(
                gram_out.at[it], gram_in.at[it, my_slot], gram_send.at[it, i],
                gram_recv.at[it, my_slot], {"freq": peer_x, "src_2": peer_c},
            )
            copy.start()
            pending.append(copy)
        if not last:
            far = dot_nt(both, a_ref[points : 2 * points, :])
            w_far[it] = far[:size] + far[size:]
            swap = remote(w_far.at[it], w_far_in.at[it], w_send.at[it], w_recv.at[it], other)
            swap.start()
            pending.append(swap)
            own = dot_nt(both, a_ref[0:points, :])
            own = own[:size] + own[size:]
            swap.wait_recv()
            own = own + w_far_in[it]
            value, top = encode(own)
            w_q[it] = value.astype(jnp.int16)
            w_s[it] = column_to_line(top)
            for d in offsets_far_first(n_x):
                peer = lax.rem(my_x + d, n_x)
                for i, (src, dst) in enumerate(((w_q, w_in_q), (w_s, w_in_s))):
                    copy = remote(
                        src.at[it], dst.at[it, my_x], x_send.at[it, i, d], x_recv.at[it, i, my_x],
                        {"freq": peer},
                    )
                    copy.start()
                    pending.append(copy)
            w_in_q[it, my_x] = w_q[it]
            w_in_s[it, my_x] = w_s[it]
        else:
            for copy in final:
                copy.wait_recv()
            pending.extend(final)
            for h in range(2):
                split_images(it + 1, h, 1)
        for copy in drained:
            copy.wait_send()
        for dx, dc in group:
            peer_x, peer_c = group_peer(dx, dc)
            slot = peer_x * n_c + peer_c
            remote(
                gram_out.at[it], gram_in.at[it, slot], gram_send.at[it, 0], gram_recv.at[it, slot],
                {"freq": peer_x, "src_2": peer_c},
            ).wait_recv()
        total = gram_in[it, 0]
        for p in range(1, n_x * n_c):
            total = total + gram_in[it, p]
        inv_high, inv_low = split2(inverse_factor(total * (1.0 / (G * G)), size))
        if not last:
            for d in offsets_far_first(n_x):
                peer = lax.rem(my_x + d, n_x)
                for i, dst in enumerate((w_in_q, w_in_s)):
                    remote(
                        dst.at[it, peer], dst.at[it, peer], x_send.at[it, i, d],
                        x_recv.at[it, i, peer], {"freq": peer},
                    ).wait_recv()
            total = decode(w_in_q[it, 0], w_in_s[it, 0])
            for p in range(1, n_x):
                total = total + decode(w_in_q[it, p], w_in_s[it, p])
            high, low = split2(total)
            cpl_own[it + 1] = apply_factor(inv_high, inv_low, high, low).astype(jnp.bfloat16)
            copy = remote(
                cpl_own.at[it + 1], cpl_far.at[it + 1], c_send.at[it + 1], c_recv.at[it + 1], other
            )
            copy.start()
            pending.append(copy)
        else:
            width = min(256, half)
            inv_twice = jnp.concatenate([inv_high, inv_high], axis=1)
            for c in range(2):
                slot = jnp.where(my_c == c, 0, 1)
                for j in range(2 * half // width):
                    cols = slice(j * width, (j + 1) * width)
                    start = c * 2 * half + j * width
                    out_ref[:, start : start + width] = apply_stacked(
                        inv_twice, inv_low, split[slot, :, cols]
                    )
    for copy in pending:
        copy.wait_send()


def shards(pupil_block, source_on, offsets, omega):
    points = pupil_block.shape[0]
    size = omega.shape[1]
    n_y, n_z, n_c = (lax.axis_size(name) for name in SRC)
    n_x = lax.axis_size("freq")
    rows = G // (n_x * n_c)
    freqs = rows * G
    assert n_y == n_z and n_c == 2
    tall, quarter = 2 * (size // n_y), freqs // 4
    f32, bf16, i32, i16 = jnp.float32, jnp.bfloat16, jnp.int32, jnp.int16
    vmem = pltpu.VMEM
    dma = pltpu.SemaphoreType.DMA

    def blocks(*lead):
        return [vmem((*lead, tall, quarter), i16), vmem((*lead, 1, LANES), f32)]

    scratch = [
        vmem((points, PB * PB), bf16), vmem((1, points), i32), vmem((2, points), i32),
        vmem((size, points), bf16),
        vmem((points, PB * PB), bf16), vmem((1, points), i32), vmem((2, points), i32),
        vmem((3, points, LANES), i32),
        vmem((2 * points, freqs), bf16),
        vmem((ITERS, size, points), bf16), vmem((ITERS, size, points), bf16),
        vmem((n_y, tall, quarter), i32), vmem((n_y, tall, LANES), f32),
        *blocks(ITERS, 2, n_y), *blocks(ITERS, 2, n_y), *blocks(ITERS, 2), *blocks(ITERS, 2, n_z),
        *blocks(ITERS, 2), *blocks(ITERS + 1, 2, n_y),
        vmem((2, 2 * size, freqs), bf16),
        vmem((ITERS, size // 2, LANES), f32), vmem((ITERS, n_x * n_c, size // 2, LANES), f32),
        vmem((ITERS, size, points), f32), vmem((ITERS, size, points), f32),
        vmem((ITERS, size, points), i16), vmem((ITERS, 1, LANES), f32),
        vmem((ITERS, n_x, size, points), i16), vmem((ITERS, n_x, 1, LANES), f32),
        dma((5,)), dma((5,)), dma((ITERS, 2, 6 * n_y)), dma((ITERS, 2, 6 * n_y)),
        dma((ITERS, n_x * n_c)), dma((ITERS, n_x * n_c)), dma((ITERS,)), dma((ITERS,)),
        dma((ITERS, 2, n_x)), dma((ITERS, 2, n_x)), dma((ITERS,)), dma((ITERS,)), dma((2,)), dma((2,)),
        dma((4,)), vmem((size, freqs), f32),
    ]
    out = pl.pallas_call(
        functools.partial(kernel, (n_y, n_z, n_c, n_x)),
        out_shape=jax.ShapeDtypeStruct((size, freqs * n_c), f32),
        in_specs=[pl.BlockSpec(memory_space=pltpu.HBM)] * 4,
        out_specs=pl.BlockSpec(memory_space=pltpu.VMEM),
        scratch_shapes=scratch,
        compiler_params=pltpu.CompilerParams(
            collective_id=0, has_side_effects=True, vmem_limit_bytes=14 * 1024 * 1024
        ),
    )(
        *(
            pltpu.with_memory_space_constraint(value, pltpu.HBM)
            for value in (pupil_block, source_on.reshape(1, points), offsets, omega.T)
        )
    )
    return out.T


def solution(mesh):
    split = Mesh(
        mesh.devices.reshape(8, 8, 2, mesh.shape["freq"]), ("src_0", "src_1", "src_2", "freq")
    )
    return jax.shard_map(
        shards,
        mesh=split,
        in_specs=(P(SRC, None), P(SRC), P(None, SRC), P(SRC, None)),
        out_specs=P("freq", None),
        check_vma=False,
    )
```
